512 devices in a mesh: chan: 64 (over x, z_lo, core), seg: 8 (over z_hi, y).
Axes of the slice: x: 4, y: 4, z: 16 (z_hi: 2, z_lo: 8; z = z_hi * 8 + z_lo), core: 2. Of those that a mesh axis runs over, the one named last changes fastest.
Arguments:
- raw_strain: bfloat16 [1024, 2048], P('chan', 'seg'), may hold values from -6 to 6
- w_first: bfloat16 [9, 64], replicated, may hold values from -2 to 2
- w_mid: bfloat16 [1, 9, 64, 64], replicated, may hold values from -0.375 to 0.375
- w_last: bfloat16 [9, 64], replicated, may hold values from -0.375 to 0.375
- lower_src: int32 [64], P('chan'), may hold values from 0 to 63, as said below
- upper_src: int32 [64], P('chan'), may hold values from 0 to 63, as said below
- valid_count: int32 [64], P('chan'), may hold values from 8 to 16, as said below
Outputs:
- stacked: float32 [1024, 33, 1024], P('chan', None, 'seg')
The draws below stay inside these ranges and needn't reach their ends.
Inputs may be any that keep to these rules, and one draw needn't show every extreme that they name: Taken in the order of the fibre, the blocks form one closed loop through all blocks: upper_src[lower_src[i]] = i, and no block is its own neighbour. The other neighbour in the same closed loop: lower_src[upper_src[i]] = i. The live channels of a block are its first valid_count channels; some block is fully live.
All inputs are finite; a program needn't handle non-finite values.
Results may differ from the reference program's by a relative error of at most 0.0073.
Values may be sent and summed in bfloat16 or wider, within the bound.
A program may use at most 64 MiB of HBM per device.

```python
import math
import jax
import jax.numpy as jnp
from jax import lax

C_DEV = 16
SEGS_DEV = 1
WIN = 256
NLAG = 64
FILT = 64
LAYERS = 3
KER = 3
BAND = 4
F = 128
CHANNELS = 1024
TIME = 2048
N_CHAN = 64
N_SEG = 8


def fibre_loop(key):
    order = jax.random.permutation(jax.random.fold_in(key, 17), N_CHAN)
    place = jnp.argsort(order)
    lower = order[(place - 1) % N_CHAN]
    upper = order[(place + 1) % N_CHAN]
    return (lower.astype(jnp.int32), upper.astype(jnp.int32))


def draw_lower_src(key, part):
    return fibre_loop(key)[0]


def draw_upper_src(key, part):
    return fibre_loop(key)[1]


def draw_valid_count(key, part):
    counts = jax.random.randint(jax.random.fold_in(key, 29), (N_CHAN,), C_DEV // 2, C_DEV + 1)
    full_at = jax.random.randint(jax.random.fold_in(key, 31), (), 0, N_CHAN)
    block_ids = jnp.arange(N_CHAN, dtype=jnp.int32)
    return jnp.where(block_ids == full_at, C_DEV, counts).astype(jnp.int32)


def shard_levels(stream_key, extent, cuts, smallest, top_value):
    def one(axis_at, blocks):
        heights = jax.random.uniform(jax.random.fold_in(jax.random.fold_in(stream_key, 6), axis_at), (blocks,), jnp.float32, smallest / len(cuts), top_value / len(cuts))
        return jnp.repeat(jnp.exp(heights), extent[axis_at] // blocks).reshape((-1,) + (1,) * (len(extent) - axis_at - 1))

    factor_of = one(*cuts[0])
    for cut in cuts[1:]:
        factor_of = factor_of * one(*cut)
    return factor_of


def centred(rng, extent, spread, most, split=(), held_as=jnp.bfloat16):
    loudness = shard_levels(rng, extent, split, -0.22, 0.18) if split else 1.0
    entries = jax.random.normal(rng, extent, jnp.float32) * spread * loudness
    return jnp.minimum(jnp.maximum(entries, -most), most).astype(held_as)


def setup_inputs(seed: int = 0) -> dict:
    streams_of = jax.random.split(jax.random.key(seed), 8)
    return {
        "raw_strain": centred(streams_of[0], (CHANNELS, TIME), 1.0, 6.0, ((0, 64), (1, 8))),
        "w_first": centred(streams_of[1], (KER * KER, FILT), (KER * KER) ** -0.5, 2.0),
        "w_mid": centred(streams_of[2], (LAYERS - 2, KER * KER, FILT, FILT), (KER * KER * FILT // 2) ** -0.5, 0.375),
        "w_last": centred(streams_of[3], (KER * KER, FILT), (KER * KER * FILT // 2) ** -0.5, 0.375),
        "lower_src": draw_lower_src(jax.random.fold_in(streams_of[7], 71), 0),
        "upper_src": draw_upper_src(jax.random.fold_in(streams_of[7], 71), 0),
        "valid_count": draw_valid_count(jax.random.fold_in(streams_of[7], 71), 0),
    }


top_precision = lax.Precision.HIGHEST

def conv_layer(feature, weight):
    out_rows = feature.shape[1] - KER + 1
    out_cols = feature.shape[2] - KER + 1
    acc_sum = None
    for tap_row in range(KER):
        shifted = jnp.concatenate([feature[:, tap_row:tap_row + out_rows, tap_col:tap_col + out_cols] for tap_col in range(KER)], axis=0)
        tap_weights = weight[tap_row * KER:(tap_row + 1) * KER].reshape(KER * feature.shape[0], weight.shape[2])
        tap_sum = jnp.einsum('io,irl->orl', tap_weights.astype(jnp.float32), shifted.astype(jnp.float32), precision=top_precision)
        acc_sum = tap_sum if acc_sum is None else acc_sum + tap_sum
    return acc_sum

def denoise(extended, w_first, w_mid, w_last):
    hidden = jnp.maximum(conv_layer(extended[None], w_first[:, None, :]), 0.0).astype(jnp.bfloat16)
    for layer_idx in range(w_mid.shape[0]):
        hidden = jnp.maximum(conv_layer(hidden, w_mid[layer_idx]), 0.0).astype(jnp.bfloat16)
    return conv_layer(hidden, w_last[:, :, None])[0]

def cleaned(masked, noise_est, live_mask, live_total):
    clean_rows = (masked.astype(jnp.float32) - noise_est) * live_mask
    common = lax.optimization_barrier(jnp.sum(clean_rows, axis=0, keepdims=True)) / live_total
    return (clean_rows - common) * live_mask

def dft_tables(width, bins):
    time_ids = jnp.arange(width, dtype=jnp.int32)
    freq_ids = jnp.arange(bins, dtype=jnp.int32)
    phases = time_ids[:, None] * freq_ids[None, :] % width
    angles = phases.astype(jnp.float32) * (2.0 * math.pi / width)
    return (jnp.cos(angles), -jnp.sin(angles))

def band_table(bins):
    bin_ids = jnp.arange(bins, dtype=jnp.int32)
    near_bins = jnp.abs(bin_ids[:, None] - bin_ids[None, :]) <= BAND
    return near_bins.astype(jnp.float32) / (2 * BAND + 1)

def lag_table(width, bins, lags, lag_scale):
    freq_ids = jnp.arange(bins, dtype=jnp.int32)
    shifts = jnp.arange(lags, dtype=jnp.int32) - lags // 2
    phases = jnp.remainder(freq_ids[:, None] * shifts[None, :], width)
    angles = phases.astype(jnp.float32) * (2.0 * math.pi / width)
    gains = jnp.where(freq_ids == 0, 1.0, 2.0).astype(jnp.float32)[:, None] * lag_scale
    return jnp.concatenate([gains * jnp.cos(angles), -gains * jnp.sin(angles)], axis=0)

def whiten(frames, width, bins):
    cos_table, sin_table = dft_tables(width, bins)
    real_part = jnp.dot(frames, cos_table, precision=top_precision)
    imag_part = jnp.dot(frames, sin_table, precision=top_precision)
    power_bins = real_part * real_part + imag_part * imag_part
    smooth = jnp.dot(power_bins, band_table(bins), precision=top_precision)
    mean_power = lax.optimization_barrier(jnp.mean(power_bins, axis=1, keepdims=True))
    divisor = jnp.sqrt(smooth + 0.1 * mean_power + 1e-06)
    return ((real_part / divisor).astype(jnp.bfloat16), (imag_part / divisor).astype(jnp.bfloat16))

def reference(raw_strain, w_first, w_mid, w_last, lower_src, upper_src, valid_count):
    seg_all = SEGS_DEV * N_SEG
    blocks = raw_strain.reshape(N_CHAN, C_DEV, TIME)
    chan_ids = jnp.arange(C_DEV, dtype=jnp.int32)
    live_mask = (chan_ids[None, :] < valid_count[:, None]).astype(jnp.bfloat16)
    masked = blocks * live_mask[:, :, None]
    padded = jnp.pad(masked, ((0, 0), (0, 0), (LAYERS, LAYERS)))
    lower_rows = jnp.take(padded, lower_src, axis=0)[:, C_DEV - LAYERS:]
    upper_rows = jnp.take(padded, upper_src, axis=0)[:, :LAYERS]
    extended = jnp.concatenate([lower_rows, padded, upper_rows], axis=1)

    def one_block(items):
        ext_rows, masked_rows, mask_rows, valid_one = items
        noise_est = denoise(ext_rows, w_first, w_mid, w_last)
        return cleaned(masked_rows, noise_est, mask_rows, valid_one.astype(jnp.float32))
    detrended = lax.map(one_block, (extended, masked, live_mask.astype(jnp.float32)[:, :, None], valid_count))
    real_part, imag_part = whiten(detrended.reshape(N_CHAN * C_DEV * seg_all, WIN), WIN, F)
    spectra = jnp.stack([real_part.reshape(N_CHAN, C_DEV, seg_all, F), imag_part.reshape(N_CHAN, C_DEV, seg_all, F)]).astype(jnp.float32)
    lag_weights = lag_table(WIN, F, NLAG, 1.0 / math.sqrt(seg_all * F))

    def per_offset(offset):
        partner = jnp.take(spectra, (jnp.arange(N_CHAN, dtype=jnp.int32) + offset) % N_CHAN, axis=1)
        products = jnp.einsum('pnasf,qnbsf->pnaqbf', spectra, partner, precision=top_precision)
        real_sum = products[0, :, :, 0] + products[1, :, :, 1]
        imag_sum = products[1, :, :, 0] - products[0, :, :, 1]
        stacked_parts = jnp.concatenate([real_sum, imag_sum], axis=3)
        lagged = jnp.dot(stacked_parts.reshape(-1, 2 * F), lag_weights, precision=top_precision)
        return lagged.reshape(N_CHAN, C_DEV, C_DEV * NLAG)
    per_all = lax.map(per_offset, jnp.arange(N_CHAN // 2 + 1, dtype=jnp.int32))
    return jnp.transpose(per_all, (1, 2, 0, 3)).reshape(N_CHAN * C_DEV, N_CHAN // 2 + 1, C_DEV * NLAG)
```

```python
import functools
import math

import jax
import jax.numpy as jnp
import numpy as np
from jax import lax
from jax.experimental import pallas as pl
from jax.experimental.pallas import tpu as pltpu
from jax.sharding import PartitionSpec as P

WIN = 256
NLAG = 64
FILT = 64
BAND = 4
F = 128
C = 16
TPAD = 264
MESH = pl.DeviceIdType.MESH
F32 = jnp.float32
BF16 = jnp.bfloat16


def split_bf16(table):
    hi = np.asarray(table, np.float32).astype(BF16)
    lo = (np.asarray(table, np.float32) - hi.astype(np.float32)).astype(BF16)
    return hi, lo


def dft_table():
    phases = np.arange(WIN)[:, None] * np.arange(F)[None, :] % WIN
    angles = phases * (2.0 * math.pi / WIN)
    return np.concatenate([np.cos(angles), -np.sin(angles)], axis=1)


def lag_table(partners, scale):
    phases = (np.arange(F)[:, None] * (np.arange(NLAG)[None, :] - NLAG // 2)) % WIN
    angles = phases * (2.0 * math.pi / WIN)
    gains = np.where(np.arange(F) == 0, 1.0, 2.0)[:, None] * scale
    one = np.concatenate([gains * np.cos(angles), -gains * np.sin(angles)], axis=0)
    return np.kron(np.eye(partners), one)


def dot(a, b):
    return jnp.dot(a, b, preferred_element_type=F32)


def build_weights(w_first, w_mid, w_last, w1f, w1, wm, w3):
    first = w_first[...].astype(F32)
    w1f[...] = jnp.zeros(w1f.shape, F32)
    for qq in range(3):
        taps = jnp.concatenate([first[3 * p + qq : 3 * p + qq + 1] for p in range(3)], axis=0)
        for late in range(3):
            for row in range(20):
                at = (late + qq) * 24 + row
                w1f[at : at + 3, late * 1280 + row * 64 : late * 1280 + row * 64 + 64] = taps
    w1[...] = w1f[...].astype(BF16)
    wm[...] = jnp.zeros(wm.shape, BF16)
    for q in range(3):
        for j in range(4):
            for p in range(3):
                wm[q, (j + p) * 64 : (j + p + 1) * 64, j * 64 : (j + 1) * 64] = w_mid[0, 3 * p + q]
    last = jnp.concatenate([w_last[...].astype(F32), jnp.zeros((9, 64), F32)], axis=1)
    last = jnp.concatenate([last, jnp.zeros((7, 128), F32)], axis=0)
    taps_t = jnp.transpose(last)[:64]
    lane = lax.broadcasted_iota(jnp.int32, (64, 128), 1)
    for q in range(3):
        base = jnp.zeros((64, 128), F32)
        for p in range(3):
            col = jnp.broadcast_to(taps_t[:, 3 * p + q : 3 * p + q + 1], (64, 128))
            base = jnp.where(lane == 2 - p, col, base)
        for row in range(18):
            rolled = pltpu.roll(base, (row - 2) % 128, axis=1)
            w3[row * 64 : (row + 1) * 64, q * 128 : (q + 1) * 128] = rolled.astype(BF16)


def convolve(ext, shifted, w1, wm, w3, h1, h2, acc):
    whole = ext[...]
    for q in range(5):
        shifted[q * 24 : (q + 1) * 24, :] = pltpu.roll(whole, (3 - q) % 384, axis=1)
    shifted[120:128, :] = jnp.zeros((8, 384), F32)
    patches = jnp.transpose(shifted[...])[:TPAD].astype(BF16)
    for block in range(15):
        cols = slice(block * 256, (block + 1) * 256)
        h1[:, cols] = jnp.maximum(dot(patches, w1[:, cols]), 0.0).astype(BF16)
    for group in range(5):
        depth, width = (384, 256) if group < 4 else (256, 128)
        total = None
        for q in range(3):
            at = q * 1280 + group * 256
            part = dot(h1[:, at : at + depth], wm[q, :depth, :width])
            total = part if total is None else total + part
        h2[:, group * 256 : group * 256 + width] = jnp.maximum(total, 0.0).astype(BF16)
    acc[...] = dot(h2[...], w3[...])
    noise_t = acc[0:256, 0:128] + acc[1:257, 128:256] + acc[2:258, 256:384]
    return jnp.transpose(noise_t)[:C]


def whiten(detrended, table_hi, table_lo):
    hi = detrended.astype(BF16)
    lo = (detrended - hi.astype(F32)).astype(BF16)
    spec = dot(hi, table_hi[...]) + (dot(lo, table_hi[...]) + dot(hi, table_lo[...]))
    re, im = spec[:, :F], spec[:, F:]
    power = re * re + im * im
    lane = lax.broadcasted_iota(jnp.int32, (C, F), 1)
    smooth = power
    for by in range(1, BAND + 1):
        smooth = smooth + jnp.where(lane >= by, pltpu.roll(power, by, axis=1), 0.0)
        smooth = smooth + jnp.where(lane < F - by, pltpu.roll(power, F - by, axis=1), 0.0)
    mean = jnp.sum(power, axis=1, keepdims=True) * (1.0 / F)
    divisor = jnp.sqrt(smooth * (1.0 / (2 * BAND + 1)) + 0.1 * mean + 1e-6)
    return jnp.concatenate([re / divisor, im / divisor], axis=1).astype(BF16)


def kernel(
    dims, raw, w_first, w_mid, w_last, lower, upper, valid, dft_hi, dft_lo, lag_hi, lag_lo, out,
    masked, packet, zbuf, xsend, xbuf, strip, own_l, own_r, strip_l, strip_r,
    w1f, w1, wm, w3, ext, shifted, h1, h2, acc, spec, xall, xf, mine, got, gf, lhs,
    z_send, z_recv, x_send, x_recv, h_send, h_recv, s_send, s_recv, c_send, c_recv,
):
    n_chan, n_seg, n_x = dims
    n_r = n_chan // n_x
    half = n_chan // 2
    partners = C // n_seg
    chan, seg = lax.axis_index("chan"), lax.axis_index("seg")
    slab = lax.div(chan, n_r)
    place = lax.rem(chan, n_r)

    def z_peer(k):
        return slab * n_r + lax.rem(place + k, n_r)

    def x_peer(k):
        return lax.rem(slab + k, n_x) * n_r + place

    def seg_peer(k):
        return lax.rem(seg + k, n_seg)

    barrier = pltpu.get_barrier_semaphore()

    def greet(peer_of, count, along):
        def one(k, carry):
            to = (peer_of(k), seg) if along == "chan" else (chan, peer_of(k))
            pl.semaphore_signal(barrier, inc=1, device_id=to, device_id_type=MESH)
            return carry
        lax.fori_loop(1, count, one, 0)

    greet(z_peer, n_r, "chan")
    greet(x_peer, n_x, "chan")
    greet(seg_peer, n_seg, "seg")

    live = (lax.broadcasted_iota(jnp.int32, (C, WIN), 0) < valid[0]).astype(F32)
    own = raw[...].astype(F32) * live
    masked[...] = own.astype(BF16)
    row8 = lax.broadcasted_iota(jnp.int32, (8, WIN), 0)
    outer = jnp.concatenate([own[13:16], own[0:3], own[0:2]], axis=0)
    outer = jnp.where(row8 == 6, upper[0].astype(F32), outer)
    outer = jnp.where(row8 == 7, lower[0].astype(F32), outer)
    packet[...] = outer.astype(BF16)
    zbuf[place] = outer.astype(BF16)

    pl.semaphore_wait(barrier, n_r + n_x + n_seg - 3)

    def z_copy(k):
        return pltpu.make_async_remote_copy(
            packet, zbuf.at[place], z_send.at[k], z_recv.at[k],
            device_id=(z_peer(k), seg), device_id_type=MESH,
        )

    def x_copy(k):
        return pltpu.make_async_remote_copy(
            xsend.at[k], xbuf.at[k], x_send.at[k], x_recv.at[k],
            device_id=(x_peer(k), seg), device_id_type=MESH,
        )

    def halo_copy(which):
        source, target, step = [
            (masked.at[:, 0:128], own_r, n_seg - 1),
            (masked.at[:, 128:256], own_l, 1),
            (strip.at[:, 0:128], strip_r, n_seg - 1),
            (strip.at[:, 128:256], strip_l, 1),
        ][which]
        return pltpu.make_async_remote_copy(
            source, target, h_send.at[which], h_recv.at[which],
            device_id=(chan, seg_peer(step)), device_id_type=MESH,
        )

    def each(first, last, act):
        def one(k, carry):
            act(k)
            return carry
        lax.fori_loop(first, last, one, 0)

    each(1, n_r, lambda k: z_copy(k).start())
    halo_copy(0).start()
    halo_copy(1).start()

    build_weights(w_first, w_mid, w_last, w1f, w1, wm, w3)

    each(1, n_r, lambda k: z_copy(k).wait_recv())
    wanted = [x_peer(k).astype(F32) for k in range(n_x)]
    picked = [jnp.zeros((8, WIN), F32) for _ in range(n_x)]
    for source in range(n_r):
        values = zbuf[source].astype(F32)
        goes = jnp.where(
            row8 < 3,
            jnp.broadcast_to(values[6:7], (8, WIN)),
            jnp.broadcast_to(values[7:8], (8, WIN)),
        )
        picked = [p + jnp.where(goes == w, values, 0.0) for p, w in zip(picked, wanted)]
    for k in range(1, n_x):
        xsend[k] = picked[k].astype(BF16)
        x_copy(k).start()
    strips = picked[0]
    for k in range(1, n_x):
        x_copy(k).wait_recv()
        strips = strips + xbuf[k].astype(F32)
    strip[...] = strips.astype(BF16)
    halo_copy(2).start()
    halo_copy(3).start()

    def edges(before, after, rows):
        lane = lax.broadcasted_iota(jnp.int32, (rows, 128), 1)
        has_before = (seg > 0).astype(F32)
        has_after = (seg < n_seg - 1).astype(F32)
        late = jnp.where(lane < 3, after[...].astype(F32) * has_after, 0.0)
        return jnp.where(lane >= 125, before[...].astype(F32) * has_before, late)

    halo_copy(0).wait_recv()
    halo_copy(1).wait_recv()
    ext[3:19, 0:256] = own
    ext[3:19, 256:384] = edges(own_l, own_r, C)
    ext[22:24, :] = jnp.zeros((2, 384), F32)
    halo_copy(2).wait_recv()
    halo_copy(3).wait_recv()
    strip_edge = edges(strip_l, strip_r, 8)
    ext[0:3, 0:256] = strips[0:3]
    ext[0:3, 256:384] = strip_edge[0:3]
    ext[19:22, 0:256] = strips[3:6]
    ext[19:22, 256:384] = strip_edge[3:6]

    noise = convolve(ext, shifted, w1, wm, w3, h1, h2, acc)
    clean = (own - noise) * live
    common = jnp.sum(clean, axis=0, keepdims=True) / valid[0].astype(F32)
    detrended = (clean - common) * live
    spectra = whiten(detrended, dft_hi, dft_lo)
    spec[...] = spectra
    xall[seg] = spectra

    def s_copy(k):
        return pltpu.make_async_remote_copy(
            spec, xall.at[seg], s_send.at[k], s_recv.at[k],
            device_id=(chan, seg_peer(k)), device_id_type=MESH,
        )

    each(1, n_seg, lambda k: s_copy(k).start())
    each(1, n_seg, lambda k: s_copy(k).wait_recv())

    flat = xall[...].reshape(n_seg * C, 2 * F)
    r_id = lax.broadcasted_iota(jnp.int32, (C, n_seg * C), 0)
    c_id = lax.broadcasted_iota(jnp.int32, (C, n_seg * C), 1)
    source_row = (r_id // partners) * C + seg * partners + r_id % partners
    chosen = dot((c_id == source_row).astype(F32).astype(BF16), flat).astype(BF16)
    mine[...] = chosen
    got[0] = chosen

    def c_copy(d):
        return pltpu.make_async_remote_copy(
            mine, got.at[d], c_send.at[d], c_recv.at[d],
            device_id=(lax.rem(chan + n_chan - d, n_chan), seg), device_id_type=MESH,
        )

    each(1, half + 1, lambda d: c_copy(d).start())
    xf[...] = xall[...].astype(F32)

    def correlate(d):
        gf[...] = got[d].astype(F32)
        at = pl.multiple_of(d * C, C)
        for b in range(partners):
            cr = jnp.zeros((C, F), F32)
            ci = jnp.zeros((C, F), F32)
            for w in range(n_seg):
                row = w * partners + b
                pr = jnp.broadcast_to(gf[row : row + 1, 0:F], (C, F))
                pi = jnp.broadcast_to(gf[row : row + 1, F : 2 * F], (C, F))
                ar, ai = xf[w, :, 0:F], xf[w, :, F : 2 * F]
                cr = cr + (ar * pr + ai * pi)
                ci = ci + (ai * pr - ar * pi)
            lhs[pl.ds(at, C), b * 256 : b * 256 + F] = cr
            lhs[pl.ds(at, C), b * 256 + F : b * 256 + 2 * F] = ci

    correlate(0)

    def arrived(d):
        c_copy(d).wait_recv()
        correlate(d)

    each(1, half + 1, arrived)

    chunk = next(c for c in range(11, 0, -1) if (half + 1) % c == 0)
    for start in range(0, half + 1, chunk):
        values = lhs[start * C : (start + chunk) * C, :]
        hi = values.astype(BF16)
        lo = (values - hi.astype(F32)).astype(BF16)
        lagged = dot(hi, lag_hi[...]) + (dot(lo, lag_hi[...]) + dot(hi, lag_lo[...]))
        for d in range(chunk):
            out[:, start + d, :] = lagged[d * C : (d + 1) * C]

    each(1, n_r, lambda k: z_copy(k).wait_send())
    for k in range(1, n_x):
        x_copy(k).wait_send()
    for which in range(4):
        halo_copy(which).wait_send()
    each(1, n_seg, lambda k: s_copy(k).wait_send())
    each(1, half + 1, lambda d: c_copy(d).wait_send())


def body(raw, w_first, w_mid, w_last, lower, upper, valid, dims):
    n_chan, n_seg, n_x = dims
    n_r = n_chan // n_x
    half = n_chan // 2
    partners = C // n_seg
    dft_hi, dft_lo = split_bf16(dft_table())
    lag_hi, lag_lo = split_bf16(lag_table(partners, 1.0 / math.sqrt(n_seg * F)))
    vmem = pl.BlockSpec(memory_space=pltpu.VMEM)
    smem = pl.BlockSpec(memory_space=pltpu.SMEM)
    dma = pltpu.SemaphoreType.DMA
    scratch = [
        pltpu.VMEM((C, WIN), BF16),
        pltpu.VMEM((8, WIN), BF16),
        pltpu.VMEM((n_r, 8, WIN), BF16),
        pltpu.VMEM((n_x, 8, WIN), BF16),
        pltpu.VMEM((n_x, 8, WIN), BF16),
        pltpu.VMEM((8, WIN), BF16),
        pltpu.VMEM((C, 128), BF16),
        pltpu.VMEM((C, 128), BF16),
        pltpu.VMEM((8, 128), BF16),
        pltpu.VMEM((8, 128), BF16),
        pltpu.VMEM((128, 3840), F32),
        pltpu.VMEM((128, 3840), BF16),
        pltpu.VMEM((3, 384, 256), BF16),
        pltpu.VMEM((1152, 384), BF16),
        pltpu.VMEM((24, 384), F32),
        pltpu.VMEM((128, 384), F32),
        pltpu.VMEM((TPAD, 3840), BF16),
        pltpu.VMEM((TPAD, 1152), BF16),
        pltpu.VMEM((TPAD, 384), F32),
        pltpu.VMEM((C, 2 * F), BF16),
        pltpu.VMEM((n_seg, C, 2 * F), BF16),
        pltpu.VMEM((n_seg, C, 2 * F), F32),
        pltpu.VMEM((C, 2 * F), BF16),
        pltpu.VMEM((half + 1, C, 2 * F), BF16),
        pltpu.VMEM((C, 2 * F), F32),
        pltpu.VMEM(((half + 1) * C, partners * 2 * F), F32),
        dma((n_r,)), dma((n_r,)), dma((n_x,)), dma((n_x,)), dma((4,)), dma((4,)),
        dma((n_seg,)), dma((n_seg,)), dma((half + 1,)), dma((half + 1,)),
    ]
    return pl.pallas_call(
        functools.partial(kernel, dims),
        out_shape=jax.ShapeDtypeStruct((C, half + 1, partners * NLAG), F32),
        in_specs=[vmem] * 4 + [smem] * 3 + [vmem] * 4,
        out_specs=vmem,
        scratch_shapes=scratch,
        compiler_params=pltpu.CompilerParams(
            collective_id=0, has_side_effects=True, vmem_limit_bytes=48 << 20
        ),
    )(
        raw, w_first, w_mid, w_last, lower, upper, valid,
        jnp.asarray(dft_hi), jnp.asarray(dft_lo), jnp.asarray(lag_hi), jnp.asarray(lag_lo),
    )


def solution(mesh):
    n_chan, n_seg = mesh.shape["chan"], mesh.shape["seg"]
    dims = (n_chan, n_seg, 4 if n_chan % 4 == 0 and n_chan >= 16 else 2)
    return jax.shard_map(
        functools.partial(body, dims=dims),
        mesh=mesh,
        in_specs=(P("chan", "seg"), P(), P(), P(), P("chan"), P("chan"), P("chan")),
        out_specs=P("chan", None, "seg"),
        check_vma=False,
    )
```

```python
import functools
import math

import jax
import jax.numpy as jnp
import numpy as np
from jax import lax
from jax.experimental import pallas as pl
from jax.experimental.pallas import tpu as pltpu
from jax.sharding import PartitionSpec as P

WIN = 256
NLAG = 64
FILT = 64
BAND = 4
F = 128
C = 16
TPAD = 264
MESH = pl.DeviceIdType.MESH
F32 = jnp.float32
BF16 = jnp.bfloat16


def split_bf16(table):
    hi = np.asarray(table, np.float32).astype(BF16)
    lo = (np.asarray(table, np.float32) - hi.astype(np.float32)).astype(BF16)
    return np.stack([hi, lo])


def dft_table():
    phases = np.arange(WIN)[:, None] * np.arange(F)[None, :] % WIN
    angles = phases * (2.0 * math.pi / WIN)
    return np.concatenate([np.cos(angles), -np.sin(angles)], axis=1)


def lag_table(partners, scale):
    phases = (np.arange(F)[:, None] * (np.arange(NLAG)[None, :] - NLAG // 2)) % WIN
    angles = phases * (2.0 * math.pi / WIN)
    gains = np.where(np.arange(F) == 0, 1.0, 2.0)[:, None] * scale
    one = np.concatenate([gains * np.cos(angles), -gains * np.sin(angles)], axis=0)
    return np.kron(np.eye(partners), one)


def dot(a, b):
    return jnp.dot(a, b, preferred_element_type=F32)


def build_weights(w_first, w_mid, w_last, w1f, w1, wm, w3):
    first = w_first[...].astype(F32)
    w1f[...] = jnp.zeros(w1f.shape, F32)
    for qq in range(3):
        taps = jnp.concatenate([first[3 * p + qq : 3 * p + qq + 1] for p in range(3)], axis=0)
        for late in range(3):
            for row in range(20):
                at = (late + qq) * 24 + row
                w1f[at : at + 3, late * 1280 + row * 64 : late * 1280 + row * 64 + 64] = taps
    w1[...] = w1f[...].astype(BF16)
    wm[...] = jnp.zeros(wm.shape, BF16)
    for q in range(3):
        for j in range(4):
            for p in range(3):
                wm[q, (j + p) * 64 : (j + p + 1) * 64, j * 64 : (j + 1) * 64] = w_mid[0, 3 * p + q]
    last = jnp.concatenate([w_last[...].astype(F32), jnp.zeros((9, 64), F32)], axis=1)
    last = jnp.concatenate([last, jnp.zeros((7, 128), F32)], axis=0)
    taps_t = jnp.transpose(last)[:64]
    lane = lax.broadcasted_iota(jnp.int32, (64, 128), 1)
    for q in range(3):
        base = jnp.zeros((64, 128), F32)
        for p in range(3):
            col = jnp.broadcast_to(taps_t[:, 3 * p + q : 3 * p + q + 1], (64, 128))
            base = jnp.where(lane == 2 - p, col, base)
        for row in range(18):
            rolled = pltpu.roll(base, (row - 2) % 128, axis=1)
            w3[row * 64 : (row + 1) * 64, q * 128 : (q + 1) * 128] = rolled.astype(BF16)


def convolve(ext, shifted, w1, wm, w3, h1, h2, acc):
    whole = ext[...]
    for q in range(5):
        shifted[q * 24 : (q + 1) * 24, :] = pltpu.roll(whole, (3 - q) % 384, axis=1)
    shifted[120:128, :] = jnp.zeros((8, 384), F32)
    patches = jnp.transpose(shifted[...])[:TPAD].astype(BF16)
    for block in range(15):
        cols = slice(block * 256, (block + 1) * 256)
        h1[:, cols] = jnp.maximum(dot(patches, w1[:, cols]), 0.0).astype(BF16)
    for group in range(5):
        depth, width = (384, 256) if group < 4 else (256, 128)
        total = None
        for q in range(3):
            at = q * 1280 + group * 256
            part = dot(h1[:, at : at + depth], wm[q, :depth, :width])
            total = part if total is None else total + part
        h2[:, group * 256 : group * 256 + width] = jnp.maximum(total, 0.0).astype(BF16)
    acc[...] = dot(h2[...], w3[...])
    noise_t = acc[0:256, 0:128] + acc[1:257, 128:256] + acc[2:258, 256:384]
    return jnp.transpose(noise_t)[:C]


def whiten(detrended, table_hi, table_lo):
    hi = detrended.astype(BF16)
    lo = (detrended - hi.astype(F32)).astype(BF16)
    spec = dot(hi, table_hi[...]) + (dot(lo, table_hi[...]) + dot(hi, table_lo[...]))
    re, im = spec[:, :F], spec[:, F:]
    power = re * re + im * im
    lane = lax.broadcasted_iota(jnp.int32, (C, F), 1)
    smooth = power
    for by in range(1, BAND + 1):
        smooth = smooth + jnp.where(lane >= by, pltpu.roll(power, by, axis=1), 0.0)
        smooth = smooth + jnp.where(lane < F - by, pltpu.roll(power, F - by, axis=1), 0.0)
    mean = jnp.sum(power, axis=1, keepdims=True) * (1.0 / F)
    divisor = jnp.sqrt(smooth * (1.0 / (2 * BAND + 1)) + 0.1 * mean + 1e-6)
    return jnp.concatenate([re / divisor, im / divisor], axis=1).astype(BF16)


def kernel(
    dims, raw_at, first_at, mid_at, last_at, lower_at, upper_at, valid_at, dft_at, lag_at, out,
    raw, w_first, w_mid, w_last, lower, upper, valid, dft, lag, in_sem,
    masked, packet, zbuf, edge_out, edge_in, xsend, xbuf, own_l, own_r,
    w1f, w1, wm, w3, ext, shifted, h1, h2, acc, spec, xall, xf, mine, got, gf, lhs,
    z_send, z_recv, e_send, e_recv, x_send, x_recv, h_send, h_recv, y_send, y_recv, o_send, o_recv,
    r_send, r_recv, n1_send, n1_recv, n2_send, n2_recv, b_send, b_recv,
):
    n_chan, n_seg, n_x = dims
    n_r = n_chan // n_x
    n_z = n_r // 2
    n_y = n_seg // 2
    half = n_chan // 2
    partners = C // n_seg
    rows = C // 2
    chan, seg = lax.axis_index("chan"), lax.axis_index("seg")
    slab = lax.div(chan, n_r)
    place = lax.rem(chan, n_r)
    level = lax.div(place, 2)
    core = lax.rem(place, 2)
    side = lax.div(seg, n_y)
    column = lax.rem(seg, n_y)

    def block_at(k_x, k_z, k_c):
        return (
            lax.rem(slab + k_x, n_x) * n_r + lax.rem(level + k_z, n_z) * 2 + lax.rem(core + k_c, 2)
        )

    def seg_at(k_h, k_y):
        return lax.rem(side + k_h, 2) * n_y + lax.rem(column + k_y, n_y)

    def each(first, last, act):
        def one(k, carry):
            act(k)
            return carry
        lax.fori_loop(first, last, one, 0)

    def send(source, target, sems, at, to):
        return pltpu.make_async_remote_copy(
            source, target, sems[0].at[at], sems[1].at[at], device_id=to, device_id_type=MESH
        )

    arrays = [
        (raw_at, raw), (valid_at, valid), (lower_at, lower), (upper_at, upper), (first_at, w_first),
        (mid_at, w_mid), (last_at, w_last), (dft_at, dft), (lag_at, lag),
    ]
    loads = [pltpu.make_async_copy(a, b, in_sem.at[i]) for i, (a, b) in enumerate(arrays)]
    for load in loads[:4]:
        load.start()

    barrier = pltpu.get_barrier_semaphore()

    def greet(to):
        pl.semaphore_signal(barrier, inc=1, device_id=to, device_id_type=MESH)

    for k_h in range(2):
        each(1 - k_h, n_z, lambda k: greet((block_at(0, k, 0), seg_at(k_h, 0))))
    for step in (1, n_seg - 1):
        each(0, n_z, lambda k: greet((block_at(0, k, 0), lax.rem(seg + step, n_seg))))
    for k in range(1, 2 * n_x):
        greet((block_at(k // 2, 0, k % 2), seg))
    each(1, n_y, lambda k: greet((chan, seg_at(0, k))))
    greeted = (2 * n_z - 1) + 2 * n_z + (2 * n_x - 1) + (n_y - 1)
    for load in loads[4:]:
        load.start()
    for load in loads[:4]:
        load.wait()

    live = (lax.broadcasted_iota(jnp.int32, (C, WIN), 0) < valid[0]).astype(F32)
    own = raw[...].astype(F32) * live
    masked[...] = own.astype(BF16)
    row8 = lax.broadcasted_iota(jnp.int32, (8, WIN), 0)
    goes_low, goes_high = upper[0].astype(F32), lower[0].astype(F32)
    outer = jnp.concatenate([own[13:16], own[0:3], own[0:2]], axis=0)
    outer = jnp.where(row8 == 6, goes_low, jnp.where(row8 == 7, goes_high, outer))
    packet[...] = outer.astype(BF16)
    zbuf[level] = outer.astype(BF16)
    row_t = lax.broadcasted_iota(jnp.int32, (8, 128), 0)
    lane_t = lax.broadcasted_iota(jnp.int32, (8, 128), 1)

    def packed(tile, first):
        out_rows = jnp.zeros((8, 128), F32)
        for r in range(6):
            here = (row_t == r) & (lane_t >= 4 * r) & (lane_t < 4 * r + 3)
            out_rows = jnp.where(here, pltpu.roll(tile, (4 * r - first) % 128, axis=1), out_rows)
        line = jnp.sum(out_rows, axis=0, keepdims=True)
        lane = lax.broadcasted_iota(jnp.int32, (1, 128), 1)
        return jnp.where(lane == 24, goes_low, jnp.where(lane == 25, goes_high, line))

    edge_out[0] = packed(outer[:, 128:256], 125)
    edge_out[1] = packed(outer[:, 0:128], 0)

    pl.semaphore_wait(barrier, greeted)

    def z_copy(k):
        return send(packet, zbuf.at[level], (z_send, z_recv), k, (block_at(0, k, 0), seg))

    def e_copy(way, k):
        step = 1 if way == 0 else n_seg - 1
        to = (block_at(0, k, 0), lax.rem(seg + step, n_seg))
        return send(edge_out.at[way], edge_in.at[way, level], (e_send, e_recv), way * n_z + k, to)

    def x_copy(k):
        return send(xsend.at[k], xbuf.at[k], (x_send, x_recv), k, (block_at(k // 2, 0, k % 2), seg))

    def halo_copy(way):
        source, target, step = [
            (masked.at[:, 128:256], own_l, 1),
            (masked.at[:, 0:128], own_r, n_seg - 1),
        ][way]
        return send(source, target, (h_send, h_recv), way, (chan, lax.rem(seg + step, n_seg)))

    for way in range(2):
        each(0, n_z, lambda k: e_copy(way, k).start())
    each(1, n_z, lambda k: z_copy(k).start())
    for way in range(2):
        halo_copy(way).start()

    for load in loads[4:]:
        load.wait()
    build_weights(w_first, w_mid, w_last, w1f, w1, wm, w3)
    for way in range(2):
        each(0, n_z, lambda k: e_copy(way, k).wait_recv())
    each(1, n_z, lambda k: z_copy(k).wait_recv())
    wanted = [block_at(k // 2, 0, k % 2).astype(F32) for k in range(2 * n_x)]
    picked = [jnp.zeros((8, WIN), F32) for _ in wanted]
    for source in range(n_z):
        values = zbuf[source].astype(F32)
        goes = jnp.where(
            row8 < 3,
            jnp.broadcast_to(values[6:7], (8, WIN)),
            jnp.broadcast_to(values[7:8], (8, WIN)),
        )
        picked = [p + jnp.where(goes == w, values, 0.0) for p, w in zip(picked, wanted)]
    lane_z = lax.broadcasted_iota(jnp.int32, (n_z, 128), 1)
    for way in range(2):
        lines = edge_in[way].reshape(n_z, 128)
        goes = jnp.where(
            lane_z < 12,
            jnp.broadcast_to(lines[:, 24:25], (n_z, 128)),
            jnp.broadcast_to(lines[:, 25:26], (n_z, 128)),
        )
        lines = jnp.where(lane_z < 24, lines, 0.0)
        for k, w in enumerate(wanted):
            line = jnp.sum(jnp.where(goes == w, lines, 0.0), axis=0, keepdims=True)
            line = jnp.concatenate([line, jnp.zeros((1, 128), F32)], axis=1)
            picked[k] = jnp.where(row8 == 6 + way, jnp.broadcast_to(line, (8, WIN)), picked[k])
    for k in range(1, 2 * n_x):
        xsend[k] = picked[k].astype(BF16)
        x_copy(k).start()

    has_before = (seg > 0).astype(F32)
    has_after = (seg < n_seg - 1).astype(F32)
    for way in range(2):
        halo_copy(way).wait_recv()
    lane_c = lax.broadcasted_iota(jnp.int32, (C, 128), 1)
    own_edge = jnp.where(lane_c < 3, own_r[...].astype(F32) * has_after, 0.0)
    own_edge = jnp.where(lane_c >= 125, own_l[...].astype(F32) * has_before, own_edge)
    ext[3:19, 0:256] = own
    ext[3:19, 256:384] = own_edge
    ext[22:24, :] = jnp.zeros((2, 384), F32)
    strips = picked[0]
    for k in range(1, 2 * n_x):
        x_copy(k).wait_recv()
        strips = strips + xbuf[k].astype(F32)
    before = jnp.broadcast_to(strips[6:7, 0:128] * has_before, (8, 128))
    after = jnp.broadcast_to(strips[7:8, 0:128] * has_after, (8, 128))
    strip_edge = jnp.zeros((8, 128), F32)
    for r in range(6):
        late = jnp.where(lane_t >= 125, pltpu.roll(before, 125 - 4 * r, axis=1), 0.0)
        both = jnp.where(lane_t < 3, pltpu.roll(after, (128 - 4 * r) % 128, axis=1), late)
        strip_edge = jnp.where(row_t == r, both, strip_edge)
    ext[0:3, 0:256] = strips[0:3]
    ext[0:3, 256:384] = strip_edge[0:3]
    ext[19:22, 0:256] = strips[3:6]
    ext[19:22, 256:384] = strip_edge[3:6]
    noise = convolve(ext, shifted, w1, wm, w3, h1, h2, acc)
    clean = (own - noise) * live
    common = jnp.sum(clean, axis=0, keepdims=True) / valid[0].astype(F32)
    detrended = (clean - common) * live
    spectra = whiten(detrended, dft.at[0], dft.at[1])
    spec[...] = spectra
    xall[seg] = spectra
    def y_copy(k):
        return send(spec, xall.at[seg], (y_send, y_recv), k, (chan, seg_at(0, k)))

    def across_copy():
        return send(spec, xall.at[seg], (o_send, o_recv), 0, (chan, seg_at(1, 0)))

    def pass_on(k):
        window = xall.at[seg_at(1, 0)]
        return send(window, window, (o_send, o_recv), k, (chan, seg_at(0, k)))

    across_copy().start()
    each(1, n_y, lambda k: y_copy(k).start())
    each(1, n_y, lambda k: y_copy(k).wait_recv())
    flat = xall[pl.ds(side * n_y, n_y)].reshape(n_y * C, 2 * F)
    r_id = lax.broadcasted_iota(jnp.int32, (C, n_y * C), 0)
    c_id = lax.broadcasted_iota(jnp.int32, (C, n_y * C), 1)
    for_seg = (r_id // rows) * n_y + column
    inner = r_id % rows
    source_row = (inner // partners) * C + for_seg * partners + inner % partners
    chosen = dot((c_id == source_row).astype(F32).astype(BF16), flat).astype(BF16)
    mine[...] = chosen.reshape(2, rows, 2 * F)
    got[place, side] = mine[side]

    def r_copy(k_h, k):
        to_side = lax.rem(side + k_h, 2)
        return send(
            mine.at[to_side], got.at[place, side], (r_send, r_recv), k_h * n_z + k,
            (block_at(0, k, 0), seg_at(k_h, 0)),
        )

    order = sorted(range(n_z), key=lambda k: (max(k, n_z - k), k))
    for k in order:
        if k:
            r_copy(0, k).start()
        r_copy(1, k).start()

    def near_copy(at):
        slot = at * 2 + core
        return send(
            got.at[slot], got.at[n_r + slot], (n1_send, n1_recv), at, (block_at(n_x - 1, 0, 0), seg)
        )

    def far_copy(at):
        slot = at * 2 + core
        return send(
            got.at[slot], got.at[2 * n_r + slot], (n2_send, n2_recv), at,
            (block_at(n_x - 2, 0, 0), seg),
        )

    def beside_copy(k_x, at):
        slot = k_x * n_r + at * 2 + core
        return send(
            got.at[slot], got.at[slot], (b_send, b_recv), k_x * n_z + at, (block_at(0, 0, 1), seg)
        )

    for k in order:
        if k:
            r_copy(0, k).wait_recv()
        r_copy(1, k).wait_recv()
        at = lax.rem(level + n_z - k, n_z)
        near_copy(at).start()

        @pl.when(at <= level)
        def _():
            far_copy(at).start()

        @pl.when(at >= level)
        def _():
            beside_copy(0, at).start()

    across_copy().wait_recv()
    each(1, n_y, lambda k: pass_on(k).start())

    for k in order:
        at = lax.rem(level + n_z - k, n_z)
        near_copy(at).wait_recv()
        beside_copy(1, at).start()

        @pl.when(at <= level)
        def _():
            far_copy(at).wait_recv()
            beside_copy(2, at).start()

    each(1, n_y, lambda k: pass_on(k).wait_recv())
    each(level, n_z, lambda at: beside_copy(0, at).wait_recv())
    each(0, n_z, lambda at: beside_copy(1, at).wait_recv())
    each(0, level + 1, lambda at: beside_copy(2, at).wait_recv())
    xf[...] = xall[...].astype(F32)

    def correlate(d):
        gf[...] = got[place + d].astype(F32).reshape(C, 2 * F)
        at = pl.multiple_of(d * C, C)
        for b in range(partners):
            cr = jnp.zeros((C, F), F32)
            ci = jnp.zeros((C, F), F32)
            for w in range(n_seg):
                row = w * partners + b
                pr = jnp.broadcast_to(gf[row : row + 1, 0:F], (C, F))
                pi = jnp.broadcast_to(gf[row : row + 1, F : 2 * F], (C, F))
                ar, ai = xf[w, :, 0:F], xf[w, :, F : 2 * F]
                cr = cr + (ar * pr + ai * pi)
                ci = ci + (ai * pr - ar * pi)
            lhs[pl.ds(at, C), b * 256 : b * 256 + F] = cr
            lhs[pl.ds(at, C), b * 256 + F : b * 256 + 2 * F] = ci

    each(0, half + 1, correlate)
    chunk = next(c for c in range(11, 0, -1) if (half + 1) % c == 0)
    for start in range(0, half + 1, chunk):
        values = lhs[start * C : (start + chunk) * C, :]
        hi = values.astype(BF16)
        lo = (values - hi.astype(F32)).astype(BF16)
        lagged = dot(hi, lag[0]) + (dot(lo, lag[0]) + dot(hi, lag[1]))
        for d in range(chunk):
            out[start + d] = lagged[d * C : (d + 1) * C]

    for way in range(2):
        each(0, n_z, lambda k: e_copy(way, k).wait_send())
        halo_copy(way).wait_send()
    each(1, n_z, lambda k: z_copy(k).wait_send())
    for k in range(1, 2 * n_x):
        x_copy(k).wait_send()
    across_copy().wait_send()
    each(1, n_y, lambda k: y_copy(k).wait_send())
    each(1, n_y, lambda k: pass_on(k).wait_send())
    each(1, n_z, lambda k: r_copy(0, k).wait_send())
    each(0, n_z, lambda k: r_copy(1, k).wait_send())
    each(0, n_z, lambda at: near_copy(at).wait_send())
    each(0, level + 1, lambda at: far_copy(at).wait_send())
    each(level, n_z, lambda at: beside_copy(0, at).wait_send())
    each(0, n_z, lambda at: beside_copy(1, at).wait_send())
    each(0, level + 1, lambda at: beside_copy(2, at).wait_send())


def body(raw, w_first, w_mid, w_last, lower, upper, valid, dims):
    n_chan, n_seg, n_x = dims
    n_r = n_chan // n_x
    n_z = n_r // 2
    n_y = n_seg // 2
    half = n_chan // 2
    partners = C // n_seg
    dft = split_bf16(dft_table())
    lag = split_bf16(lag_table(partners, 1.0 / math.sqrt(n_seg * F)))
    dma = pltpu.SemaphoreType.DMA
    scratch = [
        pltpu.VMEM(raw.shape, BF16),
        pltpu.VMEM(w_first.shape, BF16),
        pltpu.VMEM(w_mid.shape, BF16),
        pltpu.VMEM(w_last.shape, BF16),
        pltpu.SMEM((1,), jnp.int32),
        pltpu.SMEM((1,), jnp.int32),
        pltpu.SMEM((1,), jnp.int32),
        pltpu.VMEM(dft.shape, BF16),
        pltpu.VMEM(lag.shape, BF16),
        dma((9,)),
        pltpu.VMEM((C, WIN), BF16),
        pltpu.VMEM((8, WIN), BF16),
        pltpu.VMEM((n_z, 8, WIN), BF16),
        pltpu.VMEM((2, 1, 128), F32),
        pltpu.VMEM((2, n_z, 1, 128), F32),
        pltpu.VMEM((2 * n_x, 8, WIN), BF16),
        pltpu.VMEM((2 * n_x, 8, WIN), BF16),
        pltpu.VMEM((C, 128), BF16),
        pltpu.VMEM((C, 128), BF16),
        pltpu.VMEM((128, 3840), F32),
        pltpu.VMEM((128, 3840), BF16),
        pltpu.VMEM((3, 384, 256), BF16),
        pltpu.VMEM((1152, 384), BF16),
        pltpu.VMEM((24, 384), F32),
        pltpu.VMEM((128, 384), F32),
        pltpu.VMEM((TPAD, 3840), BF16),
        pltpu.VMEM((TPAD, 1152), BF16),
        pltpu.VMEM((TPAD, 384), F32),
        pltpu.VMEM((C, 2 * F), BF16),
        pltpu.VMEM((n_seg, C, 2 * F), BF16),
        pltpu.VMEM((n_seg, C, 2 * F), F32),
        pltpu.VMEM((2, C // 2, 2 * F), BF16),
        pltpu.VMEM((3 * n_r, 2, C // 2, 2 * F), BF16),
        pltpu.VMEM((C, 2 * F), F32),
        pltpu.VMEM(((half + 1) * C, partners * 2 * F), F32),
        dma((n_z,)), dma((n_z,)), dma((2 * n_z,)), dma((2 * n_z,)), dma((2 * n_x,)), dma((2 * n_x,)),
        dma((2,)), dma((2,)), dma((n_y,)), dma((n_y,)), dma((n_y,)), dma((n_y,)),
        dma((2 * n_z,)), dma((2 * n_z,)), dma((n_z,)), dma((n_z,)), dma((n_z,)), dma((n_z,)),
        dma((3 * n_z,)), dma((3 * n_z,)),
    ]
    lagged = pl.pallas_call(
        functools.partial(kernel, dims),
        out_shape=jax.ShapeDtypeStruct((half + 1, C, partners * NLAG), F32),
        in_specs=[pl.BlockSpec(memory_space=pl.ANY)] * 9,
        out_specs=pl.BlockSpec(memory_space=pltpu.VMEM),
        scratch_shapes=scratch,
        compiler_params=pltpu.CompilerParams(
            collective_id=0, has_side_effects=True, vmem_limit_bytes=48 << 20
        ),
    )(raw, w_first, w_mid, w_last, lower, upper, valid, jnp.asarray(dft), jnp.asarray(lag))
    return jnp.transpose(lagged, (1, 0, 2))


def solution(mesh):
    n_chan, n_seg = mesh.shape["chan"], mesh.shape["seg"]
    dims = (n_chan, n_seg, 4)
    return jax.shard_map(
        functools.partial(body, dims=dims),
        mesh=mesh,
        in_specs=(P("chan", "seg"), P(), P(), P(), P("chan"), P("chan"), P("chan")),
        out_specs=P("chan", None, "seg"),
        check_vma=False,
    )
```

```python
import functools
import math

import jax
import jax.numpy as jnp
import numpy as np
from jax import lax
from jax.experimental import pallas as pl
from jax.experimental.pallas import tpu as pltpu
from jax.sharding import PartitionSpec as P

WIN = 256
NLAG = 64
FILT = 64
BAND = 4
F = 128
C = 16
TPAD = 264
MESH = pl.DeviceIdType.MESH
F32 = jnp.float32
BF16 = jnp.bfloat16


def split_bf16(table):
    hi = np.asarray(table, np.float32).astype(BF16)
    lo = (np.asarray(table, np.float32) - hi.astype(np.float32)).astype(BF16)
    return np.stack([hi, lo])


def dft_table():
    phases = np.arange(WIN)[:, None] * np.arange(F)[None, :] % WIN
    angles = phases * (2.0 * math.pi / WIN)
    return np.concatenate([np.cos(angles), -np.sin(angles)], axis=1)


def lag_table(partners, scale):
    phases = (np.arange(F)[:, None] * (np.arange(NLAG)[None, :] - NLAG // 2)) % WIN
    angles = phases * (2.0 * math.pi / WIN)
    gains = np.where(np.arange(F) == 0, 1.0, 2.0)[:, None] * scale
    one = np.concatenate([gains * np.cos(angles), -gains * np.sin(angles)], axis=0)
    return np.kron(np.eye(partners), one)


def dot(a, b):
    return jnp.dot(a, b, preferred_element_type=F32)


def build_weights(w_first, w_mid, w_last, w1f, w1, wm, w3):
    first = w_first[...].astype(F32)
    w1f[...] = jnp.zeros(w1f.shape, F32)
    for qq in range(3):
        taps = jnp.concatenate([first[3 * p + qq : 3 * p + qq + 1] for p in range(3)], axis=0)
        for late in range(3):
            for row in range(20):
                at = (late + qq) * 24 + row
                w1f[at : at + 3, late * 1280 + row * 64 : late * 1280 + row * 64 + 64] = taps
    w1[...] = w1f[...].astype(BF16)
    wm[...] = jnp.zeros(wm.shape, BF16)
    for q in range(3):
        for j in range(4):
            for p in range(3):
                wm[q, (j + p) * 64 : (j + p + 1) * 64, j * 64 : (j + 1) * 64] = w_mid[0, 3 * p + q]
    last = jnp.concatenate([w_last[...].astype(F32), jnp.zeros((9, 64), F32)], axis=1)
    last = jnp.concatenate([last, jnp.zeros((7, 128), F32)], axis=0)
    taps_t = jnp.transpose(last)[:64]
    lane = lax.broadcasted_iota(jnp.int32, (64, 128), 1)
    for q in range(3):
        base = jnp.zeros((64, 128), F32)
        for p in range(3):
            col = jnp.broadcast_to(taps_t[:, 3 * p + q : 3 * p + q + 1], (64, 128))
            base = jnp.where(lane == 2 - p, col, base)
        for row in range(18):
            rolled = pltpu.roll(base, (row - 2) % 128, axis=1)
            w3[row * 64 : (row + 1) * 64, q * 128 : (q + 1) * 128] = rolled.astype(BF16)


def convolve(ext, shifted, w1, wm, w3, h1, h2, acc):
    whole = ext[...]
    for q in range(5):
        shifted[q * 24 : (q + 1) * 24, :] = pltpu.roll(whole, (3 - q) % 384, axis=1)
    shifted[120:128, :] = jnp.zeros((8, 384), F32)
    patches = jnp.transpose(shifted[...])[:TPAD].astype(BF16)
    for block in range(15):
        cols = slice(block * 256, (block + 1) * 256)
        h1[:, cols] = jnp.maximum(dot(patches, w1[:, cols]), 0.0).astype(BF16)
    for group in range(5):
        depth, width = (384, 256) if group < 4 else (256, 128)
        total = None
        for q in range(3):
            at = q * 1280 + group * 256
            part = dot(h1[:, at : at + depth], wm[q, :depth, :width])
            total = part if total is None else total + part
        h2[:, group * 256 : group * 256 + width] = jnp.maximum(total, 0.0).astype(BF16)
    acc[...] = dot(h2[...], w3[...])
    noise_t = acc[0:256, 0:128] + acc[1:257, 128:256] + acc[2:258, 256:384]
    return jnp.transpose(noise_t)[:C]


def whiten(detrended, table_hi, table_lo):
    hi = detrended.astype(BF16)
    lo = (detrended - hi.astype(F32)).astype(BF16)
    spec = dot(hi, table_hi[...]) + (dot(lo, table_hi[...]) + dot(hi, table_lo[...]))
    re, im = spec[:, :F], spec[:, F:]
    power = re * re + im * im
    lane = lax.broadcasted_iota(jnp.int32, (C, F), 1)
    smooth = power
    for by in range(1, BAND + 1):
        smooth = smooth + jnp.where(lane >= by, pltpu.roll(power, by, axis=1), 0.0)
        smooth = smooth + jnp.where(lane < F - by, pltpu.roll(power, F - by, axis=1), 0.0)
    mean = jnp.sum(power, axis=1, keepdims=True) * (1.0 / F)
    divisor = jnp.sqrt(smooth * (1.0 / (2 * BAND + 1)) + 0.1 * mean + 1e-6)
    return jnp.concatenate([re / divisor, im / divisor], axis=1)


def kernel(
    dims, raw_at, first_at, mid_at, last_at, lower, upper, valid, dft_at, lag_at, out,
    raw, w_first, w_mid, w_last, dft, lag, in_sem,
    masked, packet, zbuf, edge_out, edge_in, xsend, xbuf, own_l, own_r,
    w1f, w1, wm, w3, ext, shifted, h1, h2, acc, spec, xall, xf, mine, got, gf, lhs,
    z_send, z_recv, e_send, e_recv, x_send, x_recv, h_send, h_recv, y_send, y_recv, o_send, o_recv,
    r_send, r_recv, n1_send, n1_recv, n2_send, n2_recv, b_send, b_recv,
):
    n_chan, n_seg, n_x = dims
    n_r = n_chan // n_x
    n_z = n_r // 2
    n_y = n_seg // 2
    half = n_chan // 2
    partners = C // n_seg
    chan, seg = lax.axis_index("chan"), lax.axis_index("seg")
    slab = lax.div(chan, n_r)
    place = lax.rem(chan, n_r)
    level = lax.div(place, 2)
    core = lax.rem(place, 2)
    side = lax.div(seg, n_y)
    column = lax.rem(seg, n_y)

    def block_at(k_x, k_z, k_c):
        return (
            lax.rem(slab + k_x, n_x) * n_r + lax.rem(level + k_z, n_z) * 2 + lax.rem(core + k_c, 2)
        )

    def seg_at(k_h, k_y):
        return lax.rem(side + k_h, 2) * n_y + lax.rem(column + k_y, n_y)

    def each(first, last, act):
        def one(k, carry):
            act(k)
            return carry
        lax.fori_loop(first, last, one, 0)

    def send(source, target, sems, at, to):
        return pltpu.make_async_remote_copy(
            source, target, sems[0].at[at], sems[1].at[at], device_id=to, device_id_type=MESH
        )

    arrays = [
        (raw_at, raw), (first_at, w_first),
        (mid_at, w_mid), (last_at, w_last), (dft_at, dft), (lag_at, lag),
    ]
    loads = [pltpu.make_async_copy(a, b, in_sem.at[i]) for i, (a, b) in enumerate(arrays)]
    for load in loads[:1]:
        load.start()

    barrier = pltpu.get_barrier_semaphore()

    def greet(to):
        pl.semaphore_signal(barrier, inc=1, device_id=to, device_id_type=MESH)

    for k_h in range(2):
        each(1 - k_h, n_z, lambda k: greet((block_at(0, k, 0), seg_at(k_h, 0))))
    for step in (1, n_seg - 1):
        each(0, n_z, lambda k: greet((block_at(0, k, 0), lax.rem(seg + step, n_seg))))
    for k in range(1, 2 * n_x):
        greet((block_at(k // 2, 0, k % 2), seg))
    each(1, n_y, lambda k: greet((chan, seg_at(0, k))))
    greeted = (2 * n_z - 1) + 2 * n_z + (2 * n_x - 1) + (n_y - 1)
    for load in loads[1:]:
        load.start()
    for load in loads[:1]:
        load.wait()

    live = (lax.broadcasted_iota(jnp.int32, (C, WIN), 0) < valid[0]).astype(F32)
    own = raw[...].astype(F32) * live
    masked[...] = own.astype(BF16)
    row8 = lax.broadcasted_iota(jnp.int32, (8, WIN), 0)
    goes_low, goes_high = upper[0].astype(F32), lower[0].astype(F32)
    outer = jnp.concatenate([own[13:16], own[0:3], own[0:2]], axis=0)
    outer = jnp.where(row8 == 6, goes_low, jnp.where(row8 == 7, goes_high, outer))
    packet[...] = outer.astype(BF16)
    zbuf[level] = outer.astype(BF16)
    row_t = lax.broadcasted_iota(jnp.int32, (8, 128), 0)
    lane_t = lax.broadcasted_iota(jnp.int32, (8, 128), 1)

    def packed(tile, first):
        out_rows = jnp.zeros((8, 128), F32)
        for r in range(6):
            here = (row_t == r) & (lane_t >= 4 * r) & (lane_t < 4 * r + 3)
            out_rows = jnp.where(here, pltpu.roll(tile, (4 * r - first) % 128, axis=1), out_rows)
        line = jnp.sum(out_rows, axis=0, keepdims=True)
        lane = lax.broadcasted_iota(jnp.int32, (1, 128), 1)
        return jnp.where(lane == 24, goes_low, jnp.where(lane == 25, goes_high, line))

    edge_out[0] = packed(outer[:, 128:256], 125)
    edge_out[1] = packed(outer[:, 0:128], 0)

    pl.semaphore_wait(barrier, greeted)

    def z_copy(k):
        return send(packet, zbuf.at[level], (z_send, z_recv), k, (block_at(0, k, 0), seg))

    def e_copy(way, k):
        step = 1 if way == 0 else n_seg - 1
        to = (block_at(0, k, 0), lax.rem(seg + step, n_seg))
        return send(edge_out.at[way], edge_in.at[way, level], (e_send, e_recv), way * n_z + k, to)

    def x_copy(k):
        return send(xsend.at[k], xbuf.at[k], (x_send, x_recv), k, (block_at(k // 2, 0, k % 2), seg))

    def halo_copy(way):
        source, target, step = [
            (masked.at[:, 128:256], own_l, 1),
            (masked.at[:, 0:128], own_r, n_seg - 1),
        ][way]
        return send(source, target, (h_send, h_recv), way, (chan, lax.rem(seg + step, n_seg)))

    for way in range(2):
        each(0, n_z, lambda k: e_copy(way, k).start())
    each(1, n_z, lambda k: z_copy(k).start())
    for way in range(2):
        halo_copy(way).start()

    for load in loads[1:]:
        load.wait()
    build_weights(w_first, w_mid, w_last, w1f, w1, wm, w3)
    for way in range(2):
        each(0, n_z, lambda k: e_copy(way, k).wait_recv())
    each(1, n_z, lambda k: z_copy(k).wait_recv())
    wanted = [block_at(k // 2, 0, k % 2).astype(F32) for k in range(2 * n_x)]
    picked = [jnp.zeros((8, WIN), F32) for _ in wanted]
    for source in range(n_z):
        values = zbuf[source].astype(F32)
        goes = jnp.where(
            row8 < 3,
            jnp.broadcast_to(values[6:7], (8, WIN)),
            jnp.broadcast_to(values[7:8], (8, WIN)),
        )
        picked = [p + jnp.where(goes == w, values, 0.0) for p, w in zip(picked, wanted)]
    lane_z = lax.broadcasted_iota(jnp.int32, (n_z, 128), 1)
    for way in range(2):
        lines = edge_in[way].reshape(n_z, 128)
        goes = jnp.where(
            lane_z < 12,
            jnp.broadcast_to(lines[:, 24:25], (n_z, 128)),
            jnp.broadcast_to(lines[:, 25:26], (n_z, 128)),
        )
        lines = jnp.where(lane_z < 24, lines, 0.0)
        for k, w in enumerate(wanted):
            line = jnp.sum(jnp.where(goes == w, lines, 0.0), axis=0, keepdims=True)
            line = jnp.concatenate([line, jnp.zeros((1, 128), F32)], axis=1)
            picked[k] = jnp.where(row8 == 6 + way, jnp.broadcast_to(line, (8, WIN)), picked[k])
    for k in range(1, 2 * n_x):
        xsend[k] = picked[k].astype(BF16)
        x_copy(k).start()

    has_before = (seg > 0).astype(F32)
    has_after = (seg < n_seg - 1).astype(F32)
    for way in range(2):
        halo_copy(way).wait_recv()
    lane_c = lax.broadcasted_iota(jnp.int32, (C, 128), 1)
    own_edge = jnp.where(lane_c < 3, own_r[...].astype(F32) * has_after, 0.0)
    own_edge = jnp.where(lane_c >= 125, own_l[...].astype(F32) * has_before, own_edge)
    ext[3:19, 0:256] = own
    ext[3:19, 256:384] = own_edge
    ext[22:24, :] = jnp.zeros((2, 384), F32)
    strips = picked[0]
    for k in range(1, 2 * n_x):
        x_copy(k).wait_recv()
        strips = strips + xbuf[k].astype(F32)
    before = jnp.broadcast_to(strips[6:7, 0:128] * has_before, (8, 128))
    after = jnp.broadcast_to(strips[7:8, 0:128] * has_after, (8, 128))
    strip_edge = jnp.zeros((8, 128), F32)
    for r in range(6):
        late = jnp.where(lane_t >= 125, pltpu.roll(before, 125 - 4 * r, axis=1), 0.0)
        both = jnp.where(lane_t < 3, pltpu.roll(after, (128 - 4 * r) % 128, axis=1), late)
        strip_edge = jnp.where(row_t == r, both, strip_edge)
    ext[0:3, 0:256] = strips[0:3]
    ext[0:3, 256:384] = strip_edge[0:3]
    ext[19:22, 0:256] = strips[3:6]
    ext[19:22, 256:384] = strip_edge[3:6]
    noise = convolve(ext, shifted, w1, wm, w3, h1, h2, acc)
    clean = (own - noise) * live
    common = jnp.sum(clean, axis=0, keepdims=True) / valid[0].astype(F32)
    detrended = (clean - common) * live
    spectra = whiten(detrended, dft.at[0], dft.at[1])
    for to in range(n_seg):
        mine[to] = spectra[to * partners : (to + 1) * partners].astype(BF16)
    spec[...] = spectra.astype(BF16)
    xall[seg] = spectra.astype(BF16)
    def y_copy(k):
        return send(spec, xall.at[seg], (y_send, y_recv), k, (chan, seg_at(0, k)))

    def across_copy():
        return send(spec, xall.at[seg], (o_send, o_recv), 0, (chan, seg_at(1, 0)))

    def pass_on(k):
        window = xall.at[seg_at(1, 0)]
        return send(window, window, (o_send, o_recv), k, (chan, seg_at(0, k)))

    got[place, seg] = mine[seg]

    def r_copy(k_s, k):
        to_seg = lax.rem(seg + k_s, n_seg)
        return send(
            mine.at[to_seg], got.at[place, seg], (r_send, r_recv), k_s * n_z + k,
            (block_at(0, k, 0), to_seg),
        )

    order = sorted(range(n_z), key=lambda k: (max(k, n_z - k), k))
    for k in reversed(order):
        each(0 if k else 1, n_seg, lambda k_s: r_copy(k_s, k).start())
    across_copy().start()
    each(1, n_y, lambda k: y_copy(k).start())
    def near_copy(at):
        slot = at * 2 + core
        return send(
            got.at[slot], got.at[n_r + slot], (n1_send, n1_recv), at, (block_at(n_x - 1, 0, 0), seg)
        )

    def far_copy(at):
        slot = at * 2 + core
        return send(
            got.at[slot], got.at[2 * n_r + slot], (n2_send, n2_recv), at,
            (block_at(n_x - 2, 0, 0), seg),
        )

    def beside_copy(k_x, at):
        slot = k_x * n_r + at * 2 + core
        return send(
            got.at[slot], got.at[slot], (b_send, b_recv), k_x * n_z + at, (block_at(0, 0, 1), seg)
        )

    def other_needs(k_x, at):
        first = level * 2 + 1 - core
        slot = k_x * n_r + at * 2 + core
        return (slot >= first) & (slot <= first + half)

    def beside(k_x, at, act):
        @pl.when(other_needs(k_x, at))
        def _():
            act(beside_copy(k_x, at))

    for k in order:
        each(0 if k else 1, n_seg, lambda k_s: r_copy(k_s, k).wait_recv())
        at = lax.rem(level + n_z - k, n_z)
        near_copy(at).start()

        @pl.when(at <= level)
        def _():
            far_copy(at).start()

        beside(0, at, lambda copy: copy.start())
    across_copy().wait_recv()
    each(1, n_y, lambda k: pass_on(k).start())

    for k in order:
        at = lax.rem(level + n_z - k, n_z)
        near_copy(at).wait_recv()
        beside(1, at, lambda copy: copy.start())

        @pl.when(at <= level)
        def _():
            far_copy(at).wait_recv()

        beside(2, at, lambda copy: copy.start())

    each(1, n_y, lambda k: y_copy(k).wait_recv())
    each(1, n_y, lambda k: pass_on(k).wait_recv())
    xf[...] = xall[...].astype(F32)
    def correlate(d):
        slot = place + d

        @pl.when(lax.rem(slot, 2) != core)
        def _():
            k_x = lax.div(slot, n_r)
            at = lax.div(lax.rem(slot, n_r), 2)
            beside_copy(k_x, at).wait_recv()

        for w in range(n_seg):
            gf[w * partners : (w + 1) * partners, :] = got[slot, w].astype(F32)
        at = pl.multiple_of(d * C, C)
        for b in range(partners):
            cr = jnp.zeros((C, F), F32)
            ci = jnp.zeros((C, F), F32)
            for w in range(n_seg):
                row = w * partners + b
                pr = jnp.broadcast_to(gf[row : row + 1, 0:F], (C, F))
                pi = jnp.broadcast_to(gf[row : row + 1, F : 2 * F], (C, F))
                ar, ai = xf[w, :, 0:F], xf[w, :, F : 2 * F]
                cr = cr + (ar * pr + ai * pi)
                ci = ci + (ai * pr - ar * pi)
            lhs[pl.ds(at, C), b * 256 : b * 256 + F] = cr
            lhs[pl.ds(at, C), b * 256 + F : b * 256 + 2 * F] = ci

    chunk = next(c for c in range(11, 0, -1) if (half + 1) % c == 0)
    for start in range(0, half + 1, chunk):
        each(start, start + chunk, correlate)
        values = lhs[start * C : (start + chunk) * C, :]
        hi = values.astype(BF16)
        lo = (values - hi.astype(F32)).astype(BF16)
        lagged = dot(hi, lag[0]) + (dot(lo, lag[0]) + dot(hi, lag[1]))
        for d in range(chunk):
            out[start + d] = lagged[d * C : (d + 1) * C]

    for way in range(2):
        each(0, n_z, lambda k: e_copy(way, k).wait_send())
        halo_copy(way).wait_send()
    each(1, n_z, lambda k: z_copy(k).wait_send())
    for k in range(1, 2 * n_x):
        x_copy(k).wait_send()
    across_copy().wait_send()
    each(1, n_y, lambda k: y_copy(k).wait_send())
    each(1, n_y, lambda k: pass_on(k).wait_send())
    for k in range(n_z):
        each(0 if k else 1, n_seg, lambda k_s: r_copy(k_s, k).wait_send())
    each(0, n_z, lambda at: near_copy(at).wait_send())
    each(0, level + 1, lambda at: far_copy(at).wait_send())
    for k_x in range(3):
        each(0, n_z, lambda at: beside(k_x, at, lambda copy: copy.wait_send()))


def body(raw, w_first, w_mid, w_last, lower, upper, valid, dims):
    n_chan, n_seg, n_x = dims
    n_r = n_chan // n_x
    n_z = n_r // 2
    n_y = n_seg // 2
    half = n_chan // 2
    partners = C // n_seg
    dft = split_bf16(dft_table())
    lag = split_bf16(lag_table(partners, 1.0 / math.sqrt(n_seg * F)))
    dma = pltpu.SemaphoreType.DMA
    scratch = [
        pltpu.VMEM(raw.shape, BF16),
        pltpu.VMEM(w_first.shape, BF16),
        pltpu.VMEM(w_mid.shape, BF16),
        pltpu.VMEM(w_last.shape, BF16),
        pltpu.VMEM(dft.shape, BF16),
        pltpu.VMEM(lag.shape, BF16),
        dma((6,)),
        pltpu.VMEM((C, WIN), BF16),
        pltpu.VMEM((8, WIN), BF16),
        pltpu.VMEM((n_z, 8, WIN), BF16),
        pltpu.VMEM((2, 1, 128), F32),
        pltpu.VMEM((2, n_z, 1, 128), F32),
        pltpu.VMEM((2 * n_x, 8, WIN), BF16),
        pltpu.VMEM((2 * n_x, 8, WIN), BF16),
        pltpu.VMEM((C, 128), BF16),
        pltpu.VMEM((C, 128), BF16),
        pltpu.VMEM((128, 3840), F32),
        pltpu.VMEM((128, 3840), BF16),
        pltpu.VMEM((3, 384, 256), BF16),
        pltpu.VMEM((1152, 384), BF16),
        pltpu.VMEM((24, 384), F32),
        pltpu.VMEM((128, 384), F32),
        pltpu.VMEM((TPAD, 3840), BF16),
        pltpu.VMEM((TPAD, 1152), BF16),
        pltpu.VMEM((TPAD, 384), F32),
        pltpu.VMEM((C, 2 * F), BF16),
        pltpu.VMEM((n_seg, C, 2 * F), BF16),
        pltpu.VMEM((n_seg, C, 2 * F), F32),
        pltpu.VMEM((n_seg, partners, 2 * F), BF16),
        pltpu.VMEM((3 * n_r, n_seg, partners, 2 * F), BF16),
        pltpu.VMEM((C, 2 * F), F32),
        pltpu.VMEM(((half + 1) * C, partners * 2 * F), F32),
        dma((n_z,)), dma((n_z,)), dma((2 * n_z,)), dma((2 * n_z,)), dma((2 * n_x,)), dma((2 * n_x,)),
        dma((2,)), dma((2,)), dma((n_y,)), dma((n_y,)), dma((n_y,)), dma((n_y,)),
        dma((n_seg * n_z,)), dma((n_seg * n_z,)), dma((n_z,)), dma((n_z,)), dma((n_z,)), dma((n_z,)),
        dma((3 * n_z,)), dma((3 * n_z,)),
    ]
    hbm = pl.BlockSpec(memory_space=pltpu.HBM)
    smem = pl.BlockSpec(memory_space=pltpu.SMEM)
    lagged = pl.pallas_call(
        functools.partial(kernel, dims),
        out_shape=jax.ShapeDtypeStruct((half + 1, C, partners * NLAG), F32),
        in_specs=[hbm] * 4 + [smem] * 3 + [hbm] * 2,
        out_specs=pl.BlockSpec(memory_space=pltpu.VMEM),
        scratch_shapes=scratch,
        compiler_params=pltpu.CompilerParams(
            collective_id=0, has_side_effects=True, vmem_limit_bytes=60 << 20
        ),
    )(raw, w_first, w_mid, w_last, lower, upper, valid, jnp.asarray(dft), jnp.asarray(lag))
    return jnp.transpose(lagged, (1, 0, 2))


def solution(mesh):
    n_chan, n_seg = mesh.shape["chan"], mesh.shape["seg"]
    dims = (n_chan, n_seg, 4)
    return jax.shard_map(
        functools.partial(body, dims=dims),
        mesh=mesh,
        in_specs=(P("chan", "seg"), P(), P(), P(), P("chan"), P("chan"), P("chan")),
        out_specs=P("chan", None, "seg"),
        check_vma=False,
    )
```

```python
import functools
import math

import jax
import jax.numpy as jnp
import numpy as np
from jax import lax
from jax.experimental import pallas as pl
from jax.experimental.pallas import tpu as pltpu
from jax.sharding import PartitionSpec as P

WIN = 256
NLAG = 64
FILT = 64
BAND = 4
F = 128
C = 16
TPAD = 264
MESH = pl.DeviceIdType.MESH
F32 = jnp.float32
BF16 = jnp.bfloat16


def split_bf16(table):
    hi = np.asarray(table, np.float32).astype(BF16)
    lo = (np.asarray(table, np.float32) - hi.astype(np.float32)).astype(BF16)
    return np.stack([hi, lo])


def dft_table():
    phases = np.arange(WIN)[:, None] * np.arange(F)[None, :] % WIN
    angles = phases * (2.0 * math.pi / WIN)
    return np.concatenate([np.cos(angles), -np.sin(angles)], axis=1)


def lag_table(partners, scale):
    phases = (np.arange(F)[:, None] * (np.arange(NLAG)[None, :] - NLAG // 2)) % WIN
    angles = phases * (2.0 * math.pi / WIN)
    gains = np.where(np.arange(F) == 0, 1.0, 2.0)[:, None] * scale
    one = np.concatenate([gains * np.cos(angles), -gains * np.sin(angles)], axis=0)
    return np.kron(np.eye(partners), one)


def dot(a, b):
    return jnp.dot(a, b, preferred_element_type=F32)


def build_weights(w_first, w_mid, w_last, w1f, w1, wm, w3):
    first = w_first[...].astype(F32)
    w1f[...] = jnp.zeros(w1f.shape, F32)
    for qq in range(3):
        taps = jnp.concatenate([first[3 * p + qq : 3 * p + qq + 1] for p in range(3)], axis=0)
        for late in range(3):
            for row in range(20):
                at = (late + qq) * 24 + row
                w1f[at : at + 3, late * 1280 + row * 64 : late * 1280 + row * 64 + 64] = taps
    w1[...] = w1f[...].astype(BF16)
    wm[...] = jnp.zeros(wm.shape, BF16)
    for q in range(3):
        for j in range(4):
            for p in range(3):
                wm[q, (j + p) * 64 : (j + p + 1) * 64, j * 64 : (j + 1) * 64] = w_mid[0, 3 * p + q]
    last = jnp.concatenate([w_last[...].astype(F32), jnp.zeros((9, 64), F32)], axis=1)
    last = jnp.concatenate([last, jnp.zeros((7, 128), F32)], axis=0)
    taps_t = jnp.transpose(last)[:64]
    lane = lax.broadcasted_iota(jnp.int32, (64, 128), 1)
    for q in range(3):
        base = jnp.zeros((64, 128), F32)
        for p in range(3):
            col = jnp.broadcast_to(taps_t[:, 3 * p + q : 3 * p + q + 1], (64, 128))
            base = jnp.where(lane == 2 - p, col, base)
        for row in range(18):
            rolled = pltpu.roll(base, (row - 2) % 128, axis=1)
            w3[row * 64 : (row + 1) * 64, q * 128 : (q + 1) * 128] = rolled.astype(BF16)


def convolve(ext, shifted, w1, wm, w3, h1, h2, acc):
    whole = ext[...]
    for q in range(5):
        shifted[q * 24 : (q + 1) * 24, :] = pltpu.roll(whole, (3 - q) % 384, axis=1)
    shifted[120:128, :] = jnp.zeros((8, 384), F32)
    patches = jnp.transpose(shifted[...])[:TPAD].astype(BF16)
    for block in range(15):
        cols = slice(block * 256, (block + 1) * 256)
        h1[:, cols] = jnp.maximum(dot(patches, w1[:, cols]), 0.0).astype(BF16)
    for group in range(5):
        depth, width = (384, 256) if group < 4 else (256, 128)
        total = None
        for q in range(3):
            at = q * 1280 + group * 256
            part = dot(h1[:, at : at + depth], wm[q, :depth, :width])
            total = part if total is None else total + part
        h2[:, group * 256 : group * 256 + width] = jnp.maximum(total, 0.0).astype(BF16)
    acc[...] = dot(h2[...], w3[...])
    noise_t = acc[0:256, 0:128] + acc[1:257, 128:256] + acc[2:258, 256:384]
    return jnp.transpose(noise_t)[:C]


def whiten(detrended, table_hi, table_lo):
    hi = detrended.astype(BF16)
    lo = (detrended - hi.astype(F32)).astype(BF16)
    spec = dot(hi, table_hi[...]) + (dot(lo, table_hi[...]) + dot(hi, table_lo[...]))
    re, im = spec[:, :F], spec[:, F:]
    power = re * re + im * im
    lane = lax.broadcasted_iota(jnp.int32, (C, F), 1)
    smooth = power
    for by in range(1, BAND + 1):
        smooth = smooth + jnp.where(lane >= by, pltpu.roll(power, by, axis=1), 0.0)
        smooth = smooth + jnp.where(lane < F - by, pltpu.roll(power, F - by, axis=1), 0.0)
    mean = jnp.sum(power, axis=1, keepdims=True) * (1.0 / F)
    divisor = jnp.sqrt(smooth * (1.0 / (2 * BAND + 1)) + 0.1 * mean + 1e-6)
    return jnp.concatenate([re / divisor, im / divisor], axis=1)


def kernel(
    dims, raw_at, first_at, mid_at, last_at, lower, upper, valid, dft_at, lag_at, out,
    raw, w_first, w_mid, w_last, dft, lag, in_sem,
    masked, packet, zbuf, edge_out, edge_in, xsend, xbuf, own_l, own_r,
    w1f, w1, wm, w3, ext, shifted, h1, h2, acc, spec, xall, xf, mine, got, gf, lhs, result, out_sem,
    z_send, z_recv, e_send, e_recv, x_send, x_recv, h_send, h_recv, y_send, y_recv, o_send, o_recv,
    r_send, r_recv, n1_send, n1_recv, n2_send, n2_recv, b_send, b_recv,
):
    n_chan, n_seg, n_x = dims
    n_r = n_chan // n_x
    n_z = n_r // 2
    n_y = n_seg // 2
    half = n_chan // 2
    partners = C // n_seg
    chan, seg = lax.axis_index("chan"), lax.axis_index("seg")
    slab = lax.div(chan, n_r)
    place = lax.rem(chan, n_r)
    level = lax.div(place, 2)
    core = lax.rem(place, 2)
    side = lax.div(seg, n_y)
    column = lax.rem(seg, n_y)

    def block_at(k_x, k_z, k_c):
        return (
            lax.rem(slab + k_x, n_x) * n_r + lax.rem(level + k_z, n_z) * 2 + lax.rem(core + k_c, 2)
        )

    def seg_at(k_h, k_y):
        return lax.rem(side + k_h, 2) * n_y + lax.rem(column + k_y, n_y)

    def each(first, last, act):
        def one(k, carry):
            act(k)
            return carry
        lax.fori_loop(first, last, one, 0)

    def send(source, target, sems, at, to):
        if at is None:
            sent, landed = (sem.at[i] for sem, i in sems)
        else:
            sent, landed = (sem.at[at] for sem in sems)
        return pltpu.make_async_remote_copy(
            source, target, sent, landed, device_id=to, device_id_type=MESH
        )

    def all_of(ref, sem):
        pltpu.make_async_copy(ref, ref, sem).wait()

    arrays = [
        (raw_at, raw), (first_at, w_first),
        (mid_at, w_mid), (last_at, w_last), (dft_at, dft), (lag_at, lag),
    ]
    loads = [pltpu.make_async_copy(a, b, in_sem.at[i]) for i, (a, b) in enumerate(arrays)]
    for load in loads[:1]:
        load.start()

    barrier = pltpu.get_barrier_semaphore()

    def greet(to):
        pl.semaphore_signal(barrier, inc=1, device_id=to, device_id_type=MESH)

    for k_h in range(2):
        each(1 - k_h, n_z, lambda k: greet((block_at(0, k, 0), seg_at(k_h, 0))))
    for step in (1, n_seg - 1):
        each(0, n_z, lambda k: greet((block_at(0, k, 0), lax.rem(seg + step, n_seg))))
    for k in range(1, 2 * n_x):
        greet((block_at(k // 2, 0, k % 2), seg))
    each(1, n_y, lambda k: greet((chan, seg_at(0, k))))
    greeted = (2 * n_z - 1) + 2 * n_z + (2 * n_x - 1) + (n_y - 1)
    for load in loads[1:]:
        load.start()
    for load in loads[:1]:
        load.wait()

    live = (lax.broadcasted_iota(jnp.int32, (C, WIN), 0) < valid[0]).astype(F32)
    own = raw[...].astype(F32) * live
    masked[...] = own.astype(BF16)
    row8 = lax.broadcasted_iota(jnp.int32, (8, WIN), 0)
    goes_low, goes_high = upper[0].astype(F32), lower[0].astype(F32)
    outer = jnp.concatenate([own[13:16], own[0:3], own[0:2]], axis=0)
    outer = jnp.where(row8 == 6, goes_low, jnp.where(row8 == 7, goes_high, outer))
    packet[...] = outer.astype(BF16)
    zbuf[level] = outer.astype(BF16)
    row_t = lax.broadcasted_iota(jnp.int32, (8, 128), 0)
    lane_t = lax.broadcasted_iota(jnp.int32, (8, 128), 1)

    def packed(tile, first):
        out_rows = jnp.zeros((8, 128), F32)
        for r in range(6):
            here = (row_t == r) & (lane_t >= 4 * r) & (lane_t < 4 * r + 3)
            out_rows = jnp.where(here, pltpu.roll(tile, (4 * r - first) % 128, axis=1), out_rows)
        line = jnp.sum(out_rows, axis=0, keepdims=True)
        lane = lax.broadcasted_iota(jnp.int32, (1, 128), 1)
        return jnp.where(lane == 24, goes_low, jnp.where(lane == 25, goes_high, line))

    edge_out[0] = packed(outer[:, 128:256], 125)
    edge_out[1] = packed(outer[:, 0:128], 0)

    pl.semaphore_wait(barrier, greeted)

    def z_copy(k):
        return send(packet, zbuf.at[level], (z_send, z_recv), 0, (block_at(0, k, 0), seg))

    def e_copy(way, k):
        step = 1 if way == 0 else n_seg - 1
        to = (block_at(0, k, 0), lax.rem(seg + step, n_seg))
        return send(edge_out.at[way], edge_in.at[way, level], (e_send, e_recv), way, to)

    def x_copy(k):
        return send(xsend.at[k], xbuf.at[k], (x_send, x_recv), 0, (block_at(k // 2, 0, k % 2), seg))

    def halo_copy(way):
        source, target, step = [
            (masked.at[:, 128:256], own_l, 1),
            (masked.at[:, 0:128], own_r, n_seg - 1),
        ][way]
        return send(source, target, (h_send, h_recv), way, (chan, lax.rem(seg + step, n_seg)))

    for way in range(2):
        each(0, n_z, lambda k: e_copy(way, k).start())
    each(1, n_z, lambda k: z_copy(k).start())
    for way in range(2):
        halo_copy(way).start()

    for load in loads[1:]:
        load.wait()
    build_weights(w_first, w_mid, w_last, w1f, w1, wm, w3)
    for way in range(2):
        all_of(edge_in.at[way], e_recv.at[way])
    all_of(zbuf.at[0 : n_z - 1], z_recv.at[0])
    wanted = [block_at(k // 2, 0, k % 2).astype(F32) for k in range(2 * n_x)]
    picked = [jnp.zeros((8, WIN), F32) for _ in wanted]
    for source in range(n_z):
        values = zbuf[source].astype(F32)
        goes = jnp.where(
            row8 < 3,
            jnp.broadcast_to(values[6:7], (8, WIN)),
            jnp.broadcast_to(values[7:8], (8, WIN)),
        )
        picked = [p + jnp.where(goes == w, values, 0.0) for p, w in zip(picked, wanted)]
    lane_z = lax.broadcasted_iota(jnp.int32, (n_z, 128), 1)
    for way in range(2):
        lines = edge_in[way].reshape(n_z, 128)
        goes = jnp.where(
            lane_z < 12,
            jnp.broadcast_to(lines[:, 24:25], (n_z, 128)),
            jnp.broadcast_to(lines[:, 25:26], (n_z, 128)),
        )
        lines = jnp.where(lane_z < 24, lines, 0.0)
        for k, w in enumerate(wanted):
            line = jnp.sum(jnp.where(goes == w, lines, 0.0), axis=0, keepdims=True)
            line = jnp.concatenate([line, jnp.zeros((1, 128), F32)], axis=1)
            picked[k] = jnp.where(row8 == 6 + way, jnp.broadcast_to(line, (8, WIN)), picked[k])
    for k in range(1, 2 * n_x):
        xsend[k] = picked[k].astype(BF16)
        x_copy(k).start()

    has_before = (seg > 0).astype(F32)
    has_after = (seg < n_seg - 1).astype(F32)
    for way in range(2):
        halo_copy(way).wait_recv()
    lane_c = lax.broadcasted_iota(jnp.int32, (C, 128), 1)
    own_edge = jnp.where(lane_c < 3, own_r[...].astype(F32) * has_after, 0.0)
    own_edge = jnp.where(lane_c >= 125, own_l[...].astype(F32) * has_before, own_edge)
    ext[3:19, 0:256] = own
    ext[3:19, 256:384] = own_edge
    ext[22:24, :] = jnp.zeros((2, 384), F32)
    strips = picked[0]
    all_of(xbuf.at[1 : 2 * n_x], x_recv.at[0])
    for k in range(1, 2 * n_x):
        strips = strips + xbuf[k].astype(F32)
    before = jnp.broadcast_to(strips[6:7, 0:128] * has_before, (8, 128))
    after = jnp.broadcast_to(strips[7:8, 0:128] * has_after, (8, 128))
    strip_edge = jnp.zeros((8, 128), F32)
    for r in range(6):
        late = jnp.where(lane_t >= 125, pltpu.roll(before, 125 - 4 * r, axis=1), 0.0)
        both = jnp.where(lane_t < 3, pltpu.roll(after, (128 - 4 * r) % 128, axis=1), late)
        strip_edge = jnp.where(row_t == r, both, strip_edge)
    ext[0:3, 0:256] = strips[0:3]
    ext[0:3, 256:384] = strip_edge[0:3]
    ext[19:22, 0:256] = strips[3:6]
    ext[19:22, 256:384] = strip_edge[3:6]
    noise = convolve(ext, shifted, w1, wm, w3, h1, h2, acc)
    clean = (own - noise) * live
    common = jnp.sum(clean, axis=0, keepdims=True) / valid[0].astype(F32)
    detrended = (clean - common) * live
    spectra = whiten(detrended, dft.at[0], dft.at[1])
    for to in range(n_seg):
        mine[to] = spectra[to * partners : (to + 1) * partners].astype(BF16)
    spec[...] = spectra.astype(BF16)
    xall[seg] = spectra.astype(BF16)
    def y_copy(k):
        return send(spec, xall.at[seg], (y_send, y_recv), 0, (chan, seg_at(0, k)))

    def across_copy():
        return send(spec, xall.at[seg], (o_send, o_recv), 0, (chan, seg_at(1, 0)))

    def pass_on(k):
        window = xall.at[seg_at(1, 0)]
        return send(window, window, (o_send, o_recv), 1, (chan, seg_at(0, k)))

    got[place, seg] = mine[seg]

    def r_copy(k_s, k):
        to_seg = lax.rem(seg + k_s, n_seg)
        return send(
            mine.at[to_seg], got.at[place, seg], (r_send, r_recv), k,
            (block_at(0, k, 0), to_seg),
        )

    order = sorted(range(n_z), key=lambda k: (max(k, n_z - k), k))
    for k in reversed(order):
        each(0 if k else 1, n_seg, lambda k_s: r_copy(k_s, k).start())
    across_copy().start()
    each(1, n_y, lambda k: y_copy(k).start())
    def near_copy(at):
        slot = at * 2 + core
        return send(
            got.at[slot], got.at[n_r + slot], ((n1_send, 0), (n1_recv, at)), None, (block_at(n_x - 1, 0, 0), seg)
        )

    def far_copy(at):
        slot = at * 2 + core
        return send(
            got.at[slot], got.at[2 * n_r + slot], ((n2_send, 0), (n2_recv, at)), None,
            (block_at(n_x - 2, 0, 0), seg),
        )

    def beside_copy(k_x, at):
        slot = k_x * n_r + at * 2 + core
        return send(
            got.at[slot], got.at[slot], ((b_send, k_x), (b_recv, k_x * n_z + at)), None,
            (block_at(0, 0, 1), seg),
        )

    def other_needs(k_x, at):
        first = level * 2 + 1 - core
        slot = k_x * n_r + at * 2 + core
        return (slot >= first) & (slot <= first + half)

    def beside(k_x, at, act):
        @pl.when(other_needs(k_x, at))
        def _():
            act(beside_copy(k_x, at))

    for k in order:
        at = lax.rem(level + n_z - k, n_z)
        whole = got.at[at * 2 + core]
        all_of(whole if k else got.at[place, 0 : n_seg - 1], r_recv.at[k])
        near_copy(at).start()

        @pl.when(at <= level)
        def _():
            far_copy(at).start()

        beside(0, at, lambda copy: copy.start())
    across_copy().wait_recv()
    each(1, n_y, lambda k: pass_on(k).start())

    for k in order:
        at = lax.rem(level + n_z - k, n_z)
        near_copy(at).wait_recv()
        beside(1, at, lambda copy: copy.start())

        @pl.when(at <= level)
        def _():
            far_copy(at).wait_recv()

        beside(2, at, lambda copy: copy.start())

    if n_y > 1:
        all_of(xall.at[0 : n_y - 1], y_recv.at[0])
        all_of(xall.at[0 : n_y - 1], o_recv.at[1])
    xf[...] = xall[...].astype(F32)
    def correlate(d):
        slot = place + d

        @pl.when(lax.rem(slot, 2) != core)
        def _():
            k_x = lax.div(slot, n_r)
            at = lax.div(lax.rem(slot, n_r), 2)
            beside_copy(k_x, at).wait_recv()

        for w in range(n_seg):
            gf[w * partners : (w + 1) * partners, :] = got[slot, w].astype(F32)
        at = pl.multiple_of(d * C, C)
        for b in range(partners):
            cr = jnp.zeros((C, F), F32)
            ci = jnp.zeros((C, F), F32)
            for w in range(n_seg):
                row = w * partners + b
                pr = jnp.broadcast_to(gf[row : row + 1, 0:F], (C, F))
                pi = jnp.broadcast_to(gf[row : row + 1, F : 2 * F], (C, F))
                ar, ai = xf[w, :, 0:F], xf[w, :, F : 2 * F]
                cr = cr + (ar * pr + ai * pi)
                ci = ci + (ai * pr - ar * pi)
            lhs[pl.ds(at, C), b * 256 : b * 256 + F] = cr
            lhs[pl.ds(at, C), b * 256 + F : b * 256 + 2 * F] = ci

    stores = []
    chunk = next(c for c in range(11, 0, -1) if (half + 1) % c == 0)
    for start in range(0, half + 1, chunk):
        each(start, start + chunk, correlate)
        values = lhs[start * C : (start + chunk) * C, :]
        hi = values.astype(BF16)
        lo = (values - hi.astype(F32)).astype(BF16)
        lagged = dot(hi, lag[0]) + (dot(lo, lag[0]) + dot(hi, lag[1]))
        for d in range(chunk):
            result[start + d] = lagged[d * C : (d + 1) * C]
        part = pl.ds(start, chunk)
        stores.append(
            pltpu.make_async_copy(result.at[part], out.at[part], out_sem.at[len(stores)])
        )
        stores[-1].start()

    for way in range(2):
        all_of(edge_in.at[way], e_send.at[way])
        halo_copy(way).wait_send()
    all_of(zbuf.at[0 : n_z - 1], z_send.at[0])
    all_of(xsend.at[1 : 2 * n_x], x_send.at[0])
    across_copy().wait_send()
    if n_y > 1:
        all_of(xall.at[0 : n_y - 1], y_send.at[0])
        all_of(xall.at[0 : n_y - 1], o_send.at[1])
    for k in range(n_z):
        all_of(mine if k else mine.at[0 : n_seg - 1], r_send.at[k])
    all_of(got.at[0:n_z], n1_send.at[0])
    each(0, level + 1, lambda at: far_copy(at).wait_send())
    for k_x in range(3):
        each(0, n_z, lambda at: beside(k_x, at, lambda copy: copy.wait_send()))
    for store in stores:
        store.wait()


def body(raw, w_first, w_mid, w_last, lower, upper, valid, dims):
    n_chan, n_seg, n_x = dims
    n_r = n_chan // n_x
    n_z = n_r // 2
    n_y = n_seg // 2
    half = n_chan // 2
    partners = C // n_seg
    dft = split_bf16(dft_table())
    lag = split_bf16(lag_table(partners, 1.0 / math.sqrt(n_seg * F)))
    dma = pltpu.SemaphoreType.DMA
    chunk = next(c for c in range(11, 0, -1) if (half + 1) % c == 0)
    chunks = (half + 1) // chunk
    scratch = [
        pltpu.VMEM(raw.shape, BF16),
        pltpu.VMEM(w_first.shape, BF16),
        pltpu.VMEM(w_mid.shape, BF16),
        pltpu.VMEM(w_last.shape, BF16),
        pltpu.VMEM(dft.shape, BF16),
        pltpu.VMEM(lag.shape, BF16),
        dma((6,)),
        pltpu.VMEM((C, WIN), BF16),
        pltpu.VMEM((8, WIN), BF16),
        pltpu.VMEM((n_z, 8, WIN), BF16),
        pltpu.VMEM((2, 1, 128), F32),
        pltpu.VMEM((2, n_z, 1, 128), F32),
        pltpu.VMEM((2 * n_x, 8, WIN), BF16),
        pltpu.VMEM((2 * n_x, 8, WIN), BF16),
        pltpu.VMEM((C, 128), BF16),
        pltpu.VMEM((C, 128), BF16),
        pltpu.VMEM((128, 3840), F32),
        pltpu.VMEM((128, 3840), BF16),
        pltpu.VMEM((3, 384, 256), BF16),
        pltpu.VMEM((1152, 384), BF16),
        pltpu.VMEM((24, 384), F32),
        pltpu.VMEM((128, 384), F32),
        pltpu.VMEM((TPAD, 3840), BF16),
        pltpu.VMEM((TPAD, 1152), BF16),
        pltpu.VMEM((TPAD, 384), F32),
        pltpu.VMEM((C, 2 * F), BF16),
        pltpu.VMEM((n_seg, C, 2 * F), BF16),
        pltpu.VMEM((n_seg, C, 2 * F), F32),
        pltpu.VMEM((n_seg, partners, 2 * F), BF16),
        pltpu.VMEM((3 * n_r, n_seg, partners, 2 * F), BF16),
        pltpu.VMEM((C, 2 * F), F32),
        pltpu.VMEM(((half + 1) * C, partners * 2 * F), F32),
        pltpu.VMEM((half + 1, C, partners * NLAG), F32),
        dma((chunks,)),
        dma((1,)), dma((1,)), dma((2,)), dma((2,)), dma((1,)), dma((1,)),
        dma((2,)), dma((2,)), dma((1,)), dma((1,)), dma((2,)), dma((2,)),
        dma((n_z,)), dma((n_z,)), dma((1,)), dma((n_z,)), dma((1,)), dma((n_z,)),
        dma((3,)), dma((3 * n_z,)),
    ]
    hbm = pl.BlockSpec(memory_space=pltpu.HBM)
    smem = pl.BlockSpec(memory_space=pltpu.SMEM)
    lagged = pl.pallas_call(
        functools.partial(kernel, dims),
        out_shape=jax.ShapeDtypeStruct((half + 1, C, partners * NLAG), F32),
        in_specs=[hbm] * 4 + [smem] * 3 + [hbm] * 2,
        out_specs=hbm,
        scratch_shapes=scratch,
        compiler_params=pltpu.CompilerParams(
            collective_id=0, has_side_effects=True, vmem_limit_bytes=60 << 20
        ),
    )(raw, w_first, w_mid, w_last, lower, upper, valid, jnp.asarray(dft), jnp.asarray(lag))
    return jnp.transpose(lagged, (1, 0, 2))


def solution(mesh):
    n_chan, n_seg = mesh.shape["chan"], mesh.shape["seg"]
    dims = (n_chan, n_seg, 4)
    return jax.shard_map(
        functools.partial(body, dims=dims),
        mesh=mesh,
        in_specs=(P("chan", "seg"), P(), P(), P(), P("chan"), P("chan"), P("chan")),
        out_specs=P("chan", None, "seg"),
        check_vma=False,
    )
```

```python
import functools
import math

import jax
import jax.numpy as jnp
import numpy as np
from jax import lax
from jax.experimental import pallas as pl
from jax.experimental.pallas import tpu as pltpu
from jax.sharding import PartitionSpec as P

WIN = 256
NLAG = 64
FILT = 64
BAND = 4
F = 128
C = 16
TPAD = 264
MESH = pl.DeviceIdType.MESH
F32 = jnp.float32
BF16 = jnp.bfloat16


def split_bf16(table):
    hi = np.asarray(table, np.float32).astype(BF16)
    lo = (np.asarray(table, np.float32) - hi.astype(np.float32)).astype(BF16)
    return np.stack([hi, lo])


def dft_table():
    phases = np.arange(WIN)[:, None] * np.arange(F)[None, :] % WIN
    angles = phases * (2.0 * math.pi / WIN)
    return np.concatenate([np.cos(angles), -np.sin(angles)], axis=1)


def lag_table(partners, scale):
    phases = (np.arange(F)[:, None] * (np.arange(NLAG)[None, :] - NLAG // 2)) % WIN
    angles = phases * (2.0 * math.pi / WIN)
    gains = np.where(np.arange(F) == 0, 1.0, 2.0)[:, None] * scale
    one = np.concatenate([gains * np.cos(angles), -gains * np.sin(angles)], axis=0)
    return np.kron(np.eye(partners), one)


def dot(a, b):
    return jnp.dot(a, b, preferred_element_type=F32)


def build_weights(w_first, w_mid, w_last, w1f, w1, wm, w3):
    first = w_first[...].astype(F32)
    w1f[...] = jnp.zeros(w1f.shape, F32)
    for qq in range(3):
        taps = jnp.concatenate([first[3 * p + qq : 3 * p + qq + 1] for p in range(3)], axis=0)
        for late in range(3):
            for row in range(20):
                at = (late + qq) * 24 + row
                w1f[at : at + 3, late * 1280 + row * 64 : late * 1280 + row * 64 + 64] = taps
    w1[...] = w1f[...].astype(BF16)
    wm[...] = jnp.zeros(wm.shape, BF16)
    for q in range(3):
        for j in range(4):
            for p in range(3):
                wm[q, (j + p) * 64 : (j + p + 1) * 64, j * 64 : (j + 1) * 64] = w_mid[0, 3 * p + q]
    last = jnp.concatenate([w_last[...].astype(F32), jnp.zeros((9, 64), F32)], axis=1)
    last = jnp.concatenate([last, jnp.zeros((7, 128), F32)], axis=0)
    taps_t = jnp.transpose(last)[:64]
    lane = lax.broadcasted_iota(jnp.int32, (64, 128), 1)
    for q in range(3):
        base = jnp.zeros((64, 128), F32)
        for p in range(3):
            col = jnp.broadcast_to(taps_t[:, 3 * p + q : 3 * p + q + 1], (64, 128))
            base = jnp.where(lane == 2 - p, col, base)
        for row in range(18):
            rolled = pltpu.roll(base, (row - 2) % 128, axis=1)
            w3[row * 64 : (row + 1) * 64, q * 128 : (q + 1) * 128] = rolled.astype(BF16)


def convolve(ext, shifted, w1, wm, w3, h1, h2, acc):
    whole = ext[...]
    for q in range(5):
        shifted[q * 24 : (q + 1) * 24, :] = pltpu.roll(whole, (3 - q) % 384, axis=1)
    shifted[120:128, :] = jnp.zeros((8, 384), F32)
    patches = jnp.transpose(shifted[...])[:TPAD].astype(BF16)
    for block in range(15):
        cols = slice(block * 256, (block + 1) * 256)
        h1[:, cols] = jnp.maximum(dot(patches, w1[:, cols]), 0.0).astype(BF16)
    for group in range(5):
        depth, width = (384, 256) if group < 4 else (256, 128)
        total = None
        for q in range(3):
            at = q * 1280 + group * 256
            part = dot(h1[:, at : at + depth], wm[q, :depth, :width])
            total = part if total is None else total + part
        h2[:, group * 256 : group * 256 + width] = jnp.maximum(total, 0.0).astype(BF16)
    acc[...] = dot(h2[...], w3[...])
    noise_t = acc[0:256, 0:128] + acc[1:257, 128:256] + acc[2:258, 256:384]
    return jnp.transpose(noise_t)[:C]


def whiten(detrended, table_hi, table_lo):
    hi = detrended.astype(BF16)
    lo = (detrended - hi.astype(F32)).astype(BF16)
    spec = dot(hi, table_hi[...]) + (dot(lo, table_hi[...]) + dot(hi, table_lo[...]))
    re, im = spec[:, :F], spec[:, F:]
    power = re * re + im * im
    lane = lax.broadcasted_iota(jnp.int32, (C, F), 1)
    smooth = power
    for by in range(1, BAND + 1):
        smooth = smooth + jnp.where(lane >= by, pltpu.roll(power, by, axis=1), 0.0)
        smooth = smooth + jnp.where(lane < F - by, pltpu.roll(power, F - by, axis=1), 0.0)
    mean = jnp.sum(power, axis=1, keepdims=True) * (1.0 / F)
    divisor = jnp.sqrt(smooth * (1.0 / (2 * BAND + 1)) + 0.1 * mean + 1e-6)
    return jnp.concatenate([re / divisor, im / divisor], axis=1)


def kernel(
    dims, raw_at, first_at, mid_at, last_at, lower, upper, valid, dft_at, lag_at, out,
    raw, w_first, w_mid, w_last, dft, lag, in_sem,
    masked, packet, zbuf, edge_out, edge_in, xsend, xbuf, own_l, own_r,
    w1f, w1, wm, w3, ext, shifted, h1, h2, acc, spec, xall, xf, mine, got, gf, lhs,
    z_send, z_recv, e_send, e_recv, x_send, x_recv, h_send, h_recv, y_send, y_recv, o_send, o_recv,
    r_send, r_recv, n1_send, n1_recv, n2_send, n2_recv, b_send, b_recv,
):
    n_chan, n_seg, n_x = dims
    n_r = n_chan // n_x
    n_z = n_r // 2
    n_y = n_seg // 2
    half = n_chan // 2
    partners = C // n_seg
    chan, seg = lax.axis_index("chan"), lax.axis_index("seg")
    slab = lax.div(chan, n_r)
    place = lax.rem(chan, n_r)
    level = lax.div(place, 2)
    core = lax.rem(place, 2)
    side = lax.div(seg, n_y)
    column = lax.rem(seg, n_y)

    def block_at(k_x, k_z, k_c):
        return (
            lax.rem(slab + k_x, n_x) * n_r + lax.rem(level + k_z, n_z) * 2 + lax.rem(core + k_c, 2)
        )

    def seg_at(k_h, k_y):
        return lax.rem(side + k_h, 2) * n_y + lax.rem(column + k_y, n_y)

    def each(first, last, act):
        def one(k, carry):
            act(k)
            return carry
        lax.fori_loop(first, last, one, 0)

    def send(source, target, sems, at, to):
        if at is None:
            sent, landed = (sem.at[i] for sem, i in sems)
        else:
            sent, landed = (sem.at[at] for sem in sems)
        return pltpu.make_async_remote_copy(
            source, target, sent, landed, device_id=to, device_id_type=MESH
        )

    def all_of(ref, sem):
        pltpu.make_async_copy(ref, ref, sem).wait()

    arrays = [
        (raw_at, raw), (first_at, w_first),
        (mid_at, w_mid), (last_at, w_last), (dft_at, dft), (lag_at, lag),
    ]
    loads = [pltpu.make_async_copy(a, b, in_sem.at[i]) for i, (a, b) in enumerate(arrays)]
    for load in loads[:1]:
        load.start()

    barrier = pltpu.get_barrier_semaphore()

    def greet(to):
        pl.semaphore_signal(barrier, inc=1, device_id=to, device_id_type=MESH)

    for k_h in range(2):
        each(1 - k_h, n_z, lambda k: greet((block_at(0, k, 0), seg_at(k_h, 0))))
    for step in (1, n_seg - 1):
        each(0, n_z, lambda k: greet((block_at(0, k, 0), lax.rem(seg + step, n_seg))))
    for k in range(1, 2 * n_x):
        greet((block_at(k // 2, 0, k % 2), seg))
    each(1, n_y, lambda k: greet((chan, seg_at(0, k))))
    greeted = (2 * n_z - 1) + 2 * n_z + (2 * n_x - 1) + (n_y - 1)
    for load in loads[1:]:
        load.start()
    for load in loads[:1]:
        load.wait()

    live = (lax.broadcasted_iota(jnp.int32, (C, WIN), 0) < valid[0]).astype(F32)
    own = raw[...].astype(F32) * live
    masked[...] = own.astype(BF16)
    row8 = lax.broadcasted_iota(jnp.int32, (8, WIN), 0)
    goes_low, goes_high = upper[0].astype(F32), lower[0].astype(F32)
    outer = jnp.concatenate([own[13:16], own[0:3], own[0:2]], axis=0)
    outer = jnp.where(row8 == 6, goes_low, jnp.where(row8 == 7, goes_high, outer))
    packet[...] = outer.astype(BF16)
    zbuf[level] = outer.astype(BF16)
    row_t = lax.broadcasted_iota(jnp.int32, (8, 128), 0)
    lane_t = lax.broadcasted_iota(jnp.int32, (8, 128), 1)

    def packed(tile, first):
        out_rows = jnp.zeros((8, 128), F32)
        for r in range(6):
            here = (row_t == r) & (lane_t >= 4 * r) & (lane_t < 4 * r + 3)
            out_rows = jnp.where(here, pltpu.roll(tile, (4 * r - first) % 128, axis=1), out_rows)
        line = jnp.sum(out_rows, axis=0, keepdims=True)
        lane = lax.broadcasted_iota(jnp.int32, (1, 128), 1)
        return jnp.where(lane == 24, goes_low, jnp.where(lane == 25, goes_high, line))

    edge_out[0] = packed(outer[:, 128:256], 125)
    edge_out[1] = packed(outer[:, 0:128], 0)

    pl.semaphore_wait(barrier, greeted)

    def z_copy(k):
        return send(packet, zbuf.at[level], (z_send, z_recv), 0, (block_at(0, k, 0), seg))

    def e_copy(way, k):
        step = 1 if way == 0 else n_seg - 1
        to = (block_at(0, k, 0), lax.rem(seg + step, n_seg))
        return send(edge_out.at[way], edge_in.at[way, level], (e_send, e_recv), way, to)

    def x_copy(k):
        return send(xsend.at[k], xbuf.at[k], (x_send, x_recv), 0, (block_at(k // 2, 0, k % 2), seg))

    def halo_copy(way):
        source, target, step = [
            (masked.at[:, 128:256], own_l, 1),
            (masked.at[:, 0:128], own_r, n_seg - 1),
        ][way]
        return send(source, target, (h_send, h_recv), way, (chan, lax.rem(seg + step, n_seg)))

    for way in range(2):
        each(0, n_z, lambda k: e_copy(way, k).start())
    each(1, n_z, lambda k: z_copy(k).start())
    for way in range(2):
        halo_copy(way).start()

    for load in loads[1:]:
        load.wait()
    build_weights(w_first, w_mid, w_last, w1f, w1, wm, w3)
    for way in range(2):
        all_of(edge_in.at[way], e_recv.at[way])
    all_of(zbuf.at[0 : n_z - 1], z_recv.at[0])
    wanted = [block_at(k // 2, 0, k % 2).astype(F32) for k in range(2 * n_x)]
    picked = [jnp.zeros((8, WIN), F32) for _ in wanted]
    for source in range(n_z):
        values = zbuf[source].astype(F32)
        goes = jnp.where(
            row8 < 3,
            jnp.broadcast_to(values[6:7], (8, WIN)),
            jnp.broadcast_to(values[7:8], (8, WIN)),
        )
        picked = [p + jnp.where(goes == w, values, 0.0) for p, w in zip(picked, wanted)]
    lane_z = lax.broadcasted_iota(jnp.int32, (n_z, 128), 1)
    for way in range(2):
        lines = edge_in[way].reshape(n_z, 128)
        goes = jnp.where(
            lane_z < 12,
            jnp.broadcast_to(lines[:, 24:25], (n_z, 128)),
            jnp.broadcast_to(lines[:, 25:26], (n_z, 128)),
        )
        lines = jnp.where(lane_z < 24, lines, 0.0)
        for k, w in enumerate(wanted):
            line = jnp.sum(jnp.where(goes == w, lines, 0.0), axis=0, keepdims=True)
            line = jnp.concatenate([line, jnp.zeros((1, 128), F32)], axis=1)
            picked[k] = jnp.where(row8 == 6 + way, jnp.broadcast_to(line, (8, WIN)), picked[k])
    for k in range(1, 2 * n_x):
        xsend[k] = picked[k].astype(BF16)
        x_copy(k).start()

    has_before = (seg > 0).astype(F32)
    has_after = (seg < n_seg - 1).astype(F32)
    for way in range(2):
        halo_copy(way).wait_recv()
    lane_c = lax.broadcasted_iota(jnp.int32, (C, 128), 1)
    own_edge = jnp.where(lane_c < 3, own_r[...].astype(F32) * has_after, 0.0)
    own_edge = jnp.where(lane_c >= 125, own_l[...].astype(F32) * has_before, own_edge)
    ext[3:19, 0:256] = own
    ext[3:19, 256:384] = own_edge
    ext[22:24, :] = jnp.zeros((2, 384), F32)
    strips = picked[0]
    all_of(xbuf.at[1 : 2 * n_x], x_recv.at[0])
    for k in range(1, 2 * n_x):
        strips = strips + xbuf[k].astype(F32)
    before = jnp.broadcast_to(strips[6:7, 0:128] * has_before, (8, 128))
    after = jnp.broadcast_to(strips[7:8, 0:128] * has_after, (8, 128))
    strip_edge = jnp.zeros((8, 128), F32)
    for r in range(6):
        late = jnp.where(lane_t >= 125, pltpu.roll(before, 125 - 4 * r, axis=1), 0.0)
        both = jnp.where(lane_t < 3, pltpu.roll(after, (128 - 4 * r) % 128, axis=1), late)
        strip_edge = jnp.where(row_t == r, both, strip_edge)
    ext[0:3, 0:256] = strips[0:3]
    ext[0:3, 256:384] = strip_edge[0:3]
    ext[19:22, 0:256] = strips[3:6]
    ext[19:22, 256:384] = strip_edge[3:6]
    noise = convolve(ext, shifted, w1, wm, w3, h1, h2, acc)
    clean = (own - noise) * live
    common = jnp.sum(clean, axis=0, keepdims=True) / valid[0].astype(F32)
    detrended = (clean - common) * live
    spectra = whiten(detrended, dft.at[0], dft.at[1])
    for to in range(n_seg):
        mine[to] = spectra[to * partners : (to + 1) * partners].astype(BF16)
    spec[...] = spectra.astype(BF16)
    xall[seg] = spectra.astype(BF16)
    def y_copy(k):
        return send(spec, xall.at[seg], (y_send, y_recv), 0, (chan, seg_at(0, k)))

    def across_copy():
        return send(spec, xall.at[seg], (o_send, o_recv), 0, (chan, seg_at(1, 0)))

    def pass_on(k):
        window = xall.at[seg_at(1, 0)]
        return send(window, window, (o_send, o_recv), 1, (chan, seg_at(0, k)))

    got[place, seg] = mine[seg]

    def r_copy(k_s, k):
        to_seg = lax.rem(seg + k_s, n_seg)
        return send(
            mine.at[to_seg], got.at[place, seg], ((r_send, 0), (r_recv, k)), None,
            (block_at(0, k, 0), to_seg),
        )

    order = sorted(range(n_z), key=lambda k: (max(k, n_z - k), k))
    for k in reversed(order):
        each(0 if k else 1, n_seg, lambda k_s: r_copy(k_s, k).start())
    across_copy().start()
    each(1, n_y, lambda k: y_copy(k).start())
    def near_copy(at):
        slot = at * 2 + core
        return send(
            got.at[slot], got.at[n_r + slot], ((n1_send, 0), (n1_recv, at)), None, (block_at(n_x - 1, 0, 0), seg)
        )

    def far_copy(at):
        slot = at * 2 + core
        return send(
            got.at[slot], got.at[2 * n_r + slot], ((n2_send, 0), (n2_recv, at)), None,
            (block_at(n_x - 2, 0, 0), seg),
        )

    def beside_copy(k_x, at):
        slot = k_x * n_r + at * 2 + core
        return send(
            got.at[slot], got.at[slot], ((b_send, 0), (b_recv, k_x * n_z + at)), None,
            (block_at(0, 0, 1), seg),
        )

    def other_needs(k_x, at):
        first = level * 2 + 1 - core
        slot = k_x * n_r + at * 2 + core
        return (slot >= first) & (slot <= first + half)

    def beside(k_x, at, act):
        @pl.when(other_needs(k_x, at))
        def _():
            act(beside_copy(k_x, at))

    for k in order:
        at = lax.rem(level + n_z - k, n_z)
        whole = got.at[at * 2 + core]
        all_of(whole if k else got.at[place, 0 : n_seg - 1], r_recv.at[k])
        near_copy(at).start()

        @pl.when(at <= level)
        def _():
            far_copy(at).start()

        beside(0, at, lambda copy: copy.start())
    across_copy().wait_recv()
    each(1, n_y, lambda k: pass_on(k).start())

    for k in order:
        at = lax.rem(level + n_z - k, n_z)
        near_copy(at).wait_recv()
        beside(1, at, lambda copy: copy.start())

        @pl.when(at <= level)
        def _():
            far_copy(at).wait_recv()

        beside(2, at, lambda copy: copy.start())

    if n_y > 1:
        all_of(xall.at[0 : n_y - 1], y_recv.at[0])
        all_of(xall.at[0 : n_y - 1], o_recv.at[1])
    xf[...] = xall[...].astype(F32)
    def correlate(d):
        slot = place + d

        @pl.when(lax.rem(slot, 2) != core)
        def _():
            k_x = lax.div(slot, n_r)
            at = lax.div(lax.rem(slot, n_r), 2)
            beside_copy(k_x, at).wait_recv()

        for w in range(n_seg):
            gf[w * partners : (w + 1) * partners, :] = got[slot, w].astype(F32)
        at = pl.multiple_of(d * C, C)
        for b in range(partners):
            cr = jnp.zeros((C, F), F32)
            ci = jnp.zeros((C, F), F32)
            for w in range(n_seg):
                row = w * partners + b
                pr = jnp.broadcast_to(gf[row : row + 1, 0:F], (C, F))
                pi = jnp.broadcast_to(gf[row : row + 1, F : 2 * F], (C, F))
                ar, ai = xf[w, :, 0:F], xf[w, :, F : 2 * F]
                cr = cr + (ar * pr + ai * pi)
                ci = ci + (ai * pr - ar * pi)
            lhs[pl.ds(at, C), b * 256 : b * 256 + F] = cr
            lhs[pl.ds(at, C), b * 256 + F : b * 256 + 2 * F] = ci

    chunk = next(c for c in range(11, 0, -1) if (half + 1) % c == 0)
    for start in range(0, half + 1, chunk):
        each(start, start + chunk, correlate)
        values = lhs[start * C : (start + chunk) * C, :]
        hi = values.astype(BF16)
        lo = (values - hi.astype(F32)).astype(BF16)
        lagged = dot(hi, lag[0]) + (dot(lo, lag[0]) + dot(hi, lag[1]))
        for d in range(chunk):
            out[start + d] = lagged[d * C : (d + 1) * C]

    for way in range(2):
        all_of(edge_in.at[way], e_send.at[way])
        halo_copy(way).wait_send()
    all_of(zbuf.at[0 : n_z - 1], z_send.at[0])
    all_of(xsend.at[1 : 2 * n_x], x_send.at[0])
    across_copy().wait_send()
    if n_y > 1:
        all_of(xall.at[0 : n_y - 1], y_send.at[0])
        all_of(xall.at[0 : n_y - 1], o_send.at[1])
    for k in range(n_z):
        all_of(mine if k else mine.at[0 : n_seg - 1], r_send.at[0])
    all_of(got.at[0:n_z], n1_send.at[0])
    each(0, level + 1, lambda at: far_copy(at).wait_send())
    for k_x in range(3):
        each(0, n_z, lambda at: beside(k_x, at, lambda copy: copy.wait_send()))


def body(raw, w_first, w_mid, w_last, lower, upper, valid, dims):
    n_chan, n_seg, n_x = dims
    n_r = n_chan // n_x
    n_z = n_r // 2
    n_y = n_seg // 2
    half = n_chan // 2
    partners = C // n_seg
    dft = split_bf16(dft_table())
    lag = split_bf16(lag_table(partners, 1.0 / math.sqrt(n_seg * F)))
    dma = pltpu.SemaphoreType.DMA
    scratch = [
        pltpu.VMEM(raw.shape, BF16),
        pltpu.VMEM(w_first.shape, BF16),
        pltpu.VMEM(w_mid.shape, BF16),
        pltpu.VMEM(w_last.shape, BF16),
        pltpu.VMEM(dft.shape, BF16),
        pltpu.VMEM(lag.shape, BF16),
        dma((6,)),
        pltpu.VMEM((C, WIN), BF16),
        pltpu.VMEM((8, WIN), BF16),
        pltpu.VMEM((n_z, 8, WIN), BF16),
        pltpu.VMEM((2, 1, 128), F32),
        pltpu.VMEM((2, n_z, 1, 128), F32),
        pltpu.VMEM((2 * n_x, 8, WIN), BF16),
        pltpu.VMEM((2 * n_x, 8, WIN), BF16),
        pltpu.VMEM((C, 128), BF16),
        pltpu.VMEM((C, 128), BF16),
        pltpu.VMEM((128, 3840), F32),
        pltpu.VMEM((128, 3840), BF16),
        pltpu.VMEM((3, 384, 256), BF16),
        pltpu.VMEM((1152, 384), BF16),
        pltpu.VMEM((24, 384), F32),
        pltpu.VMEM((128, 384), F32),
        pltpu.VMEM((TPAD, 3840), BF16),
        pltpu.VMEM((TPAD, 1152), BF16),
        pltpu.VMEM((TPAD, 384), F32),
        pltpu.VMEM((C, 2 * F), BF16),
        pltpu.VMEM((n_seg, C, 2 * F), BF16),
        pltpu.VMEM((n_seg, C, 2 * F), F32),
        pltpu.VMEM((n_seg, partners, 2 * F), BF16),
        pltpu.VMEM((3 * n_r, n_seg, partners, 2 * F), BF16),
        pltpu.VMEM((C, 2 * F), F32),
        pltpu.VMEM(((half + 1) * C, partners * 2 * F), F32),
        dma((1,)), dma((1,)), dma((2,)), dma((2,)), dma((1,)), dma((1,)),
        dma((2,)), dma((2,)), dma((1,)), dma((1,)), dma((2,)), dma((2,)),
        dma((1,)), dma((n_z,)), dma((1,)), dma((n_z,)), dma((1,)), dma((n_z,)),
        dma((1,)), dma((3 * n_z,)),
    ]
    hbm = pl.BlockSpec(memory_space=pltpu.HBM)
    smem = pl.BlockSpec(memory_space=pltpu.SMEM)
    placed = [raw, w_first, w_mid, w_last, lower, upper, valid, jnp.asarray(dft), jnp.asarray(lag)]
    placed = [
        x if x.ndim == 1 else pltpu.with_memory_space_constraint(x, pltpu.HBM) for x in placed
    ]
    lagged = pl.pallas_call(
        functools.partial(kernel, dims),
        out_shape=jax.ShapeDtypeStruct((half + 1, C, partners * NLAG), F32),
        in_specs=[hbm] * 4 + [smem] * 3 + [hbm] * 2,
        out_specs=pl.BlockSpec(memory_space=pltpu.VMEM),
        scratch_shapes=scratch,
        compiler_params=pltpu.CompilerParams(
            collective_id=0, has_side_effects=True, vmem_limit_bytes=48 << 20
        ),
    )(*placed)
    return jnp.transpose(lagged, (1, 0, 2))


def solution(mesh):
    n_chan, n_seg = mesh.shape["chan"], mesh.shape["seg"]
    dims = (n_chan, n_seg, 4)
    return jax.shard_map(
        functools.partial(body, dims=dims),
        mesh=mesh,
        in_specs=(P("chan", "seg"), P(), P(), P(), P("chan"), P("chan"), P("chan")),
        out_specs=P("chan", None, "seg"),
        check_vma=False,
    )
```

```python
import functools
import math

import jax
import jax.numpy as jnp
import numpy as np
from jax import lax
from jax.experimental import pallas as pl
from jax.experimental.pallas import tpu as pltpu
from jax.sharding import PartitionSpec as P

WIN = 256
NLAG = 64
FILT = 64
BAND = 4
F = 128
C = 16
TPAD = 264
MESH = pl.DeviceIdType.MESH
F32 = jnp.float32
BF16 = jnp.bfloat16


def split_bf16(table):
    hi = np.asarray(table, np.float32).astype(BF16)
    lo = (np.asarray(table, np.float32) - hi.astype(np.float32)).astype(BF16)
    return np.stack([hi, lo])


def dft_table():
    phases = np.arange(WIN)[:, None] * np.arange(F)[None, :] % WIN
    angles = phases * (2.0 * math.pi / WIN)
    return np.concatenate([np.cos(angles), -np.sin(angles)], axis=1)


def lag_table(partners, scale):
    phases = (np.arange(F)[:, None] * (np.arange(NLAG)[None, :] - NLAG // 2)) % WIN
    angles = phases * (2.0 * math.pi / WIN)
    gains = np.where(np.arange(F) == 0, 1.0, 2.0)[:, None] * scale
    one = np.concatenate([gains * np.cos(angles), -gains * np.sin(angles)], axis=0)
    return np.kron(np.eye(partners), one)


def dot(a, b):
    return jnp.dot(a, b, preferred_element_type=F32)


def build_weights(w_first, w_mid, w_last, w1f, w1, wm, w3):
    first = w_first[...].astype(F32)
    w1f[...] = jnp.zeros(w1f.shape, F32)
    for qq in range(3):
        taps = jnp.concatenate([first[3 * p + qq : 3 * p + qq + 1] for p in range(3)], axis=0)
        for late in range(3):
            for row in range(20):
                at = (late + qq) * 24 + row
                w1f[at : at + 3, late * 1280 + row * 64 : late * 1280 + row * 64 + 64] = taps
    w1[...] = w1f[...].astype(BF16)
    wm[...] = jnp.zeros(wm.shape, BF16)
    for q in range(3):
        for j in range(4):
            for p in range(3):
                wm[q, (j + p) * 64 : (j + p + 1) * 64, j * 64 : (j + 1) * 64] = w_mid[0, 3 * p + q]
    last = jnp.concatenate([w_last[...].astype(F32), jnp.zeros((9, 64), F32)], axis=1)
    last = jnp.concatenate([last, jnp.zeros((7, 128), F32)], axis=0)
    taps_t = jnp.transpose(last)[:64]
    lane = lax.broadcasted_iota(jnp.int32, (64, 128), 1)
    for q in range(3):
        base = jnp.zeros((64, 128), F32)
        for p in range(3):
            col = jnp.broadcast_to(taps_t[:, 3 * p + q : 3 * p + q + 1], (64, 128))
            base = jnp.where(lane == 2 - p, col, base)
        for row in range(18):
            rolled = pltpu.roll(base, (row - 2) % 128, axis=1)
            w3[row * 64 : (row + 1) * 64, q * 128 : (q + 1) * 128] = rolled.astype(BF16)


def hide(ext, shifted, w1, wm, h1, h2, groups, ready):
    whole = ext[...]
    for q in range(5):
        shifted[q * 24 : (q + 1) * 24, :] = pltpu.roll(whole, (3 - q) % 384, axis=1)
    shifted[120:128, :] = jnp.zeros((8, 384), F32)
    patches = jnp.transpose(shifted[...])[:TPAD].astype(BF16)
    for group in groups:
        for late in range(3):
            at = late * 1280 + group * 256
            h1[:, at : at + 256] = jnp.maximum(dot(patches, w1[:, at : at + 256]), 0.0).astype(BF16)
    for group in ready:
        depth, width = (384, 256) if group < 4 else (256, 128)
        total = None
        for q in range(3):
            at = q * 1280 + group * 256
            part = dot(h1[:, at : at + depth], wm[q, :depth, :width])
            total = part if total is None else total + part
        h2[:, group * 256 : group * 256 + width] = jnp.maximum(total, 0.0).astype(BF16)


def whiten(detrended, table_hi, table_lo):
    hi = detrended.astype(BF16)
    lo = (detrended - hi.astype(F32)).astype(BF16)
    spec = dot(hi, table_hi[...]) + (dot(lo, table_hi[...]) + dot(hi, table_lo[...]))
    re, im = spec[:, :F], spec[:, F:]
    power = re * re + im * im
    lane = lax.broadcasted_iota(jnp.int32, (C, F), 1)
    smooth = power
    for by in range(1, BAND + 1):
        smooth = smooth + jnp.where(lane >= by, pltpu.roll(power, by, axis=1), 0.0)
        smooth = smooth + jnp.where(lane < F - by, pltpu.roll(power, F - by, axis=1), 0.0)
    mean = jnp.sum(power, axis=1, keepdims=True) * (1.0 / F)
    divisor = jnp.sqrt(smooth * (1.0 / (2 * BAND + 1)) + 0.1 * mean + 1e-6)
    return jnp.concatenate([re / divisor, im / divisor], axis=1)


def kernel(
    dims, raw_at, first_at, mid_at, last_at, lower, upper, valid, dft_at, lag_at, out,
    raw, w_first, w_mid, w_last, dft, lag, in_sem,
    masked, packet, zbuf, edge_out, edge_in, xsend, xbuf, own_l, own_r,
    w1f, w1, wm, w3, ext, shifted, h1, h2, acc, spec, xall, xf, mine, got, gf, lhs,
    z_send, z_recv, e_send, e_recv, x_send, x_recv, h_send, h_recv, y_send, y_recv, o_send, o_recv,
    r_send, r_recv, n1_send, n1_recv, n2_send, n2_recv, b_send, b_recv,
):
    n_chan, n_seg, n_x = dims
    n_r = n_chan // n_x
    n_z = n_r // 2
    n_y = n_seg // 2
    half = n_chan // 2
    partners = C // n_seg
    chan, seg = lax.axis_index("chan"), lax.axis_index("seg")
    slab = lax.div(chan, n_r)
    place = lax.rem(chan, n_r)
    level = lax.div(place, 2)
    core = lax.rem(place, 2)
    side = lax.div(seg, n_y)
    column = lax.rem(seg, n_y)

    def block_at(k_x, k_z, k_c):
        return (
            lax.rem(slab + k_x, n_x) * n_r + lax.rem(level + k_z, n_z) * 2 + lax.rem(core + k_c, 2)
        )

    def seg_at(k_h, k_y):
        return lax.rem(side + k_h, 2) * n_y + lax.rem(column + k_y, n_y)

    def each(first, last, act):
        def one(k, carry):
            act(k)
            return carry
        lax.fori_loop(first, last, one, 0)

    def send(source, target, sems, at, to):
        if at is None:
            sent, landed = (sem.at[i] for sem, i in sems)
        else:
            sent, landed = (sem.at[at] for sem in sems)
        return pltpu.make_async_remote_copy(
            source, target, sent, landed, device_id=to, device_id_type=MESH
        )

    def all_of(ref, sem):
        pltpu.make_async_copy(ref, ref, sem).wait()

    arrays = [
        (raw_at, raw), (first_at, w_first),
        (mid_at, w_mid), (last_at, w_last), (dft_at, dft), (lag_at, lag),
    ]
    loads = [pltpu.make_async_copy(a, b, in_sem.at[i]) for i, (a, b) in enumerate(arrays)]
    for load in loads[:1]:
        load.start()

    barrier = pltpu.get_barrier_semaphore()

    def greet(to):
        pl.semaphore_signal(barrier, inc=1, device_id=to, device_id_type=MESH)

    for step in (1, n_seg - 1):
        each(0, n_z, lambda k: greet((block_at(0, k, 0), lax.rem(seg + step, n_seg))))
    for k_h in range(2):
        each(1 - k_h, n_z, lambda k: greet((block_at(0, k, 0), seg_at(k_h, 0))))
    for k in range(1, 2 * n_x):
        greet((block_at(k // 2, 0, k % 2), seg))
    each(1, n_y, lambda k: greet((chan, seg_at(0, k))))
    greeted = (2 * n_z - 1) + 2 * n_z + (2 * n_x - 1) + (n_y - 1)
    for load in loads[1:]:
        load.start()
    for load in loads[:1]:
        load.wait()

    live = (lax.broadcasted_iota(jnp.int32, (C, WIN), 0) < valid[0]).astype(F32)
    own = raw[...].astype(F32) * live
    masked[...] = own.astype(BF16)
    row8 = lax.broadcasted_iota(jnp.int32, (8, WIN), 0)
    goes_low, goes_high = upper[0].astype(F32), lower[0].astype(F32)
    outer = jnp.concatenate([own[13:16], own[0:3], own[0:2]], axis=0)
    outer = jnp.where(row8 == 6, goes_low, jnp.where(row8 == 7, goes_high, outer))
    packet[...] = outer.astype(BF16)
    zbuf[level] = outer.astype(BF16)
    row_t = lax.broadcasted_iota(jnp.int32, (8, 128), 0)
    lane_t = lax.broadcasted_iota(jnp.int32, (8, 128), 1)

    def packed(tile, first):
        out_rows = jnp.zeros((8, 128), F32)
        for r in range(6):
            here = (row_t == r) & (lane_t >= 4 * r) & (lane_t < 4 * r + 3)
            out_rows = jnp.where(here, pltpu.roll(tile, (4 * r - first) % 128, axis=1), out_rows)
        line = jnp.sum(out_rows, axis=0, keepdims=True)
        lane = lax.broadcasted_iota(jnp.int32, (1, 128), 1)
        return jnp.where(lane == 24, goes_low, jnp.where(lane == 25, goes_high, line))

    edge_out[0] = packed(outer[:, 128:256], 125)
    edge_out[1] = packed(outer[:, 0:128], 0)

    pl.semaphore_wait(barrier, greeted)

    def z_copy(k):
        return send(packet, zbuf.at[level], (z_send, z_recv), 0, (block_at(0, k, 0), seg))

    def e_copy(way, k):
        step = 1 if way == 0 else n_seg - 1
        to = (block_at(0, k, 0), lax.rem(seg + step, n_seg))
        return send(edge_out.at[way], edge_in.at[way, level], (e_send, e_recv), way, to)

    def x_copy(k):
        return send(xsend.at[k], xbuf.at[k], (x_send, x_recv), 0, (block_at(k // 2, 0, k % 2), seg))

    def halo_copy(way):
        source, target, step = [
            (masked.at[:, 128:256], own_l, 1),
            (masked.at[:, 0:128], own_r, n_seg - 1),
        ][way]
        return send(source, target, (h_send, h_recv), way, (chan, lax.rem(seg + step, n_seg)))

    for way in range(2):
        each(0, n_z, lambda k: e_copy(way, k).start())
    each(1, n_z, lambda k: z_copy(k).start())
    for way in range(2):
        halo_copy(way).start()

    for load in loads[1:]:
        load.wait()
    build_weights(w_first, w_mid, w_last, w1f, w1, wm, w3)
    for way in range(2):
        all_of(edge_in.at[way], e_recv.at[way])
    all_of(zbuf.at[0 : n_z - 1], z_recv.at[0])
    wanted = [block_at(k // 2, 0, k % 2).astype(F32) for k in range(2 * n_x)]
    picked = [jnp.zeros((8, WIN), F32) for _ in wanted]
    for source in range(n_z):
        values = zbuf[source].astype(F32)
        goes = jnp.where(
            row8 < 3,
            jnp.broadcast_to(values[6:7], (8, WIN)),
            jnp.broadcast_to(values[7:8], (8, WIN)),
        )
        picked = [p + jnp.where(goes == w, values, 0.0) for p, w in zip(picked, wanted)]
    lane_z = lax.broadcasted_iota(jnp.int32, (n_z, 128), 1)
    for way in range(2):
        lines = edge_in[way].reshape(n_z, 128)
        goes = jnp.where(
            lane_z < 12,
            jnp.broadcast_to(lines[:, 24:25], (n_z, 128)),
            jnp.broadcast_to(lines[:, 25:26], (n_z, 128)),
        )
        lines = jnp.where(lane_z < 24, lines, 0.0)
        for k, w in enumerate(wanted):
            line = jnp.sum(jnp.where(goes == w, lines, 0.0), axis=0, keepdims=True)
            line = jnp.concatenate([line, jnp.zeros((1, 128), F32)], axis=1)
            picked[k] = jnp.where(row8 == 6 + way, jnp.broadcast_to(line, (8, WIN)), picked[k])
    for k in range(1, 2 * n_x):
        xsend[k] = picked[k].astype(BF16)
        x_copy(k).start()

    has_before = (seg > 0).astype(F32)
    has_after = (seg < n_seg - 1).astype(F32)
    for way in range(2):
        halo_copy(way).wait_recv()
    lane_c = lax.broadcasted_iota(jnp.int32, (C, 128), 1)
    own_edge = jnp.where(lane_c < 3, own_r[...].astype(F32) * has_after, 0.0)
    own_edge = jnp.where(lane_c >= 125, own_l[...].astype(F32) * has_before, own_edge)
    ext[3:19, 0:256] = own
    ext[3:19, 256:384] = own_edge
    ext[0:3, :] = jnp.zeros((3, 384), F32)
    ext[19:24, :] = jnp.zeros((5, 384), F32)
    hide(ext, shifted, w1, wm, h1, h2, (1, 2, 3), (1, 2))
    acc[...] = dot(h2[:, 256:768], w3[256:768])
    strips = picked[0]
    all_of(xbuf.at[1 : 2 * n_x], x_recv.at[0])
    for k in range(1, 2 * n_x):
        strips = strips + xbuf[k].astype(F32)
    before = jnp.broadcast_to(strips[6:7, 0:128] * has_before, (8, 128))
    after = jnp.broadcast_to(strips[7:8, 0:128] * has_after, (8, 128))
    strip_edge = jnp.zeros((8, 128), F32)
    for r in range(6):
        late = jnp.where(lane_t >= 125, pltpu.roll(before, 125 - 4 * r, axis=1), 0.0)
        both = jnp.where(lane_t < 3, pltpu.roll(after, (128 - 4 * r) % 128, axis=1), late)
        strip_edge = jnp.where(row_t == r, both, strip_edge)
    ext[0:3, 0:256] = strips[0:3]
    ext[0:3, 256:384] = strip_edge[0:3]
    ext[19:22, 0:256] = strips[3:6]
    ext[19:22, 256:384] = strip_edge[3:6]
    hide(ext, shifted, w1, wm, h1, h2, (0, 4), (0, 3, 4))
    acc[...] += dot(h2[:, 0:256], w3[0:256]) + dot(h2[:, 768:1152], w3[768:1152])
    noise_t = acc[0:256, 0:128] + acc[1:257, 128:256] + acc[2:258, 256:384]
    noise = jnp.transpose(noise_t)[:C]
    clean = (own - noise) * live
    common = jnp.sum(clean, axis=0, keepdims=True) / valid[0].astype(F32)
    detrended = (clean - common) * live
    spectra = whiten(detrended, dft.at[0], dft.at[1])
    for to in range(n_seg):
        mine[to] = spectra[to * partners : (to + 1) * partners].astype(BF16)
    spec[...] = spectra.astype(BF16)
    xall[seg] = spectra.astype(BF16)
    def y_copy(k):
        return send(spec, xall.at[seg], (y_send, y_recv), 0, (chan, seg_at(0, k)))

    def across_copy():
        return send(spec, xall.at[seg], (o_send, o_recv), 0, (chan, seg_at(1, 0)))

    def pass_on(k):
        window = xall.at[seg_at(1, 0)]
        return send(window, window, (o_send, o_recv), 1, (chan, seg_at(0, k)))

    got[place, seg] = mine[seg]

    def r_copy(k_s, k):
        to_seg = lax.rem(seg + k_s, n_seg)
        return send(
            mine.at[to_seg], got.at[place, seg], ((r_send, 0), (r_recv, k)), None,
            (block_at(0, k, 0), to_seg),
        )

    across_copy().start()
    each(1, n_y, lambda k: y_copy(k).start())
    order = sorted(range(n_z), key=lambda k: (max(k, n_z - k), k))
    for k in reversed(order):
        each(0 if k else 1, n_seg, lambda k_s: r_copy(k_s, k).start())
    def slab_copy(k_x, at, k_c):
        slot = at * 2 + core
        sent, landed = (n1_send, n1_recv) if k_x == 1 else (n2_send, n2_recv)
        return send(
            got.at[slot], got.at[k_x * n_r + slot], ((sent, 0), (landed, k_c * n_z + at)), None,
            (block_at(n_x - k_x, 0, k_c), seg),
        )

    def beside_copy(at):
        slot = at * 2 + core
        return send(
            got.at[slot], got.at[slot], ((b_send, 0), (b_recv, at)), None, (block_at(0, 0, 1), seg)
        )

    def other_needs(k_x, at):
        first = level * 2 + 1 - core
        slot = k_x * n_r + at * 2 + core
        return (slot >= first) & (slot <= first + half)

    def leaving(at, act):
        @pl.when(at <= level)
        def _():
            act(slab_copy(2, at, 0))

        @pl.when(other_needs(2, at))
        def _():
            act(slab_copy(2, at, 1))

        for k_c in range(2):
            act(slab_copy(1, at, k_c))

        @pl.when(other_needs(0, at))
        def _():
            act(beside_copy(at))

    for turn, k in enumerate(order):
        if turn == min(3, n_z - 1):
            across_copy().wait_recv()
            each(1, n_y, lambda k: pass_on(k).start())
        at = lax.rem(level + n_z - k, n_z)
        whole = got.at[at * 2 + core]
        all_of(whole if k else got.at[place, 0 : n_seg - 1], r_recv.at[k])
        leaving(at, lambda copy: copy.start())

    if n_y > 1:
        all_of(xall.at[0 : n_y - 1], y_recv.at[0])
        all_of(xall.at[0 : n_y - 1], o_recv.at[1])
    xf[...] = xall[...].astype(F32)
    def correlate(d):
        slot = place + d

        k_x, at = lax.div(slot, n_r), lax.div(lax.rem(slot, n_r), 2)
        apart = lax.rem(slot + core, 2)

        @pl.when((k_x == 0) & (apart == 1))
        def _():
            beside_copy(at).wait_recv()

        for far, landed in ((1, n1_recv), (2, n2_recv)):

            @pl.when(k_x == far)
            def _():
                all_of(got.at[slot], landed.at[apart * n_z + at])

        for w in range(n_seg):
            gf[w * partners : (w + 1) * partners, :] = got[slot, w].astype(F32)
        at = pl.multiple_of(d * C, C)
        for b in range(partners):
            cr = jnp.zeros((C, F), F32)
            ci = jnp.zeros((C, F), F32)
            for w in range(n_seg):
                row = w * partners + b
                pr = jnp.broadcast_to(gf[row : row + 1, 0:F], (C, F))
                pi = jnp.broadcast_to(gf[row : row + 1, F : 2 * F], (C, F))
                ar, ai = xf[w, :, 0:F], xf[w, :, F : 2 * F]
                cr = cr + (ar * pr + ai * pi)
                ci = ci + (ai * pr - ar * pi)
            lhs[pl.ds(at, C), b * 256 : b * 256 + F] = cr
            lhs[pl.ds(at, C), b * 256 + F : b * 256 + 2 * F] = ci

    chunk = next(c for c in range(11, 0, -1) if (half + 1) % c == 0)
    for start in range(0, half + 1, chunk):
        each(start, start + chunk, correlate)
        values = lhs[start * C : (start + chunk) * C, :]
        hi = values.astype(BF16)
        lo = (values - hi.astype(F32)).astype(BF16)
        lagged = dot(hi, lag[0]) + (dot(lo, lag[0]) + dot(hi, lag[1]))
        for d in range(chunk):
            out[start + d] = lagged[d * C : (d + 1) * C]

    for way in range(2):
        all_of(edge_in.at[way], e_send.at[way])
        halo_copy(way).wait_send()
    all_of(zbuf.at[0 : n_z - 1], z_send.at[0])
    all_of(xsend.at[1 : 2 * n_x], x_send.at[0])
    across_copy().wait_send()
    if n_y > 1:
        all_of(xall.at[0 : n_y - 1], y_send.at[0])
        all_of(xall.at[0 : n_y - 1], o_send.at[1])
    for k in range(n_z):
        all_of(mine if k else mine.at[0 : n_seg - 1], r_send.at[0])
    each(0, n_z, lambda at: leaving(at, lambda copy: copy.wait_send()))


def body(raw, w_first, w_mid, w_last, lower, upper, valid, dims):
    n_chan, n_seg, n_x = dims
    n_r = n_chan // n_x
    n_z = n_r // 2
    n_y = n_seg // 2
    half = n_chan // 2
    partners = C // n_seg
    dft = split_bf16(dft_table())
    lag = split_bf16(lag_table(partners, 1.0 / math.sqrt(n_seg * F)))
    dma = pltpu.SemaphoreType.DMA
    scratch = [
        pltpu.VMEM(raw.shape, BF16),
        pltpu.VMEM(w_first.shape, BF16),
        pltpu.VMEM(w_mid.shape, BF16),
        pltpu.VMEM(w_last.shape, BF16),
        pltpu.VMEM(dft.shape, BF16),
        pltpu.VMEM(lag.shape, BF16),
        dma((6,)),
        pltpu.VMEM((C, WIN), BF16),
        pltpu.VMEM((8, WIN), BF16),
        pltpu.VMEM((n_z, 8, WIN), BF16),
        pltpu.VMEM((2, 1, 128), F32),
        pltpu.VMEM((2, n_z, 1, 128), F32),
        pltpu.VMEM((2 * n_x, 8, WIN), BF16),
        pltpu.VMEM((2 * n_x, 8, WIN), BF16),
        pltpu.VMEM((C, 128), BF16),
        pltpu.VMEM((C, 128), BF16),
        pltpu.VMEM((128, 3840), F32),
        pltpu.VMEM((128, 3840), BF16),
        pltpu.VMEM((3, 384, 256), BF16),
        pltpu.VMEM((1152, 384), BF16),
        pltpu.VMEM((24, 384), F32),
        pltpu.VMEM((128, 384), F32),
        pltpu.VMEM((TPAD, 3840), BF16),
        pltpu.VMEM((TPAD, 1152), BF16),
        pltpu.VMEM((TPAD, 384), F32),
        pltpu.VMEM((C, 2 * F), BF16),
        pltpu.VMEM((n_seg, C, 2 * F), BF16),
        pltpu.VMEM((n_seg, C, 2 * F), F32),
        pltpu.VMEM((n_seg, partners, 2 * F), BF16),
        pltpu.VMEM((3 * n_r, n_seg, partners, 2 * F), BF16),
        pltpu.VMEM((C, 2 * F), F32),
        pltpu.VMEM(((half + 1) * C, partners * 2 * F), F32),
        dma((1,)), dma((1,)), dma((2,)), dma((2,)), dma((1,)), dma((1,)),
        dma((2,)), dma((2,)), dma((1,)), dma((1,)), dma((2,)), dma((2,)),
        dma((1,)), dma((n_z,)), dma((1,)), dma((2 * n_z,)), dma((1,)), dma((2 * n_z,)),
        dma((1,)), dma((n_z,)),
    ]
    hbm = pl.BlockSpec(memory_space=pltpu.HBM)
    smem = pl.BlockSpec(memory_space=pltpu.SMEM)
    placed = [raw, w_first, w_mid, w_last, lower, upper, valid, jnp.asarray(dft), jnp.asarray(lag)]
    placed = [
        x if x.ndim == 1 else pltpu.with_memory_space_constraint(x, pltpu.HBM) for x in placed
    ]
    lagged = pl.pallas_call(
        functools.partial(kernel, dims),
        out_shape=jax.ShapeDtypeStruct((half + 1, C, partners * NLAG), F32),
        in_specs=[hbm] * 4 + [smem] * 3 + [hbm] * 2,
        out_specs=pl.BlockSpec(memory_space=pltpu.VMEM),
        scratch_shapes=scratch,
        compiler_params=pltpu.CompilerParams(
            collective_id=0, has_side_effects=True, vmem_limit_bytes=48 << 20
        ),
    )(*placed)
    return jnp.transpose(lagged, (1, 0, 2))


def solution(mesh):
    n_chan, n_seg = mesh.shape["chan"], mesh.shape["seg"]
    dims = (n_chan, n_seg, 4)
    return jax.shard_map(
        functools.partial(body, dims=dims),
        mesh=mesh,
        in_specs=(P("chan", "seg"), P(), P(), P(), P("chan"), P("chan"), P("chan")),
        out_specs=P("chan", None, "seg"),
        check_vma=False,
    )
```

```python
import functools
import math

import jax
import jax.numpy as jnp
import numpy as np
from jax import lax
from jax.experimental import pallas as pl
from jax.experimental.pallas import tpu as pltpu
from jax.sharding import PartitionSpec as P

WIN = 256
NLAG = 64
FILT = 64
BAND = 4
F = 128
C = 16
TPAD = 264
MESH = pl.DeviceIdType.MESH
F32 = jnp.float32
BF16 = jnp.bfloat16


def split_bf16(table):
    hi = np.asarray(table, np.float32).astype(BF16)
    lo = (np.asarray(table, np.float32) - hi.astype(np.float32)).astype(BF16)
    return np.stack([hi, lo])


def dft_table():
    phases = np.arange(WIN)[:, None] * np.arange(F)[None, :] % WIN
    angles = phases * (2.0 * math.pi / WIN)
    return np.concatenate([np.cos(angles), -np.sin(angles)], axis=1)


def lag_table(partners, scale):
    phases = (np.arange(F)[:, None] * (np.arange(NLAG)[None, :] - NLAG // 2)) % WIN
    angles = phases * (2.0 * math.pi / WIN)
    gains = np.where(np.arange(F) == 0, 1.0, 2.0)[:, None] * scale
    one = np.concatenate([gains * np.cos(angles), -gains * np.sin(angles)], axis=0)
    return np.kron(np.eye(partners), one)


def dot(a, b):
    return jnp.dot(a, b, preferred_element_type=F32)


def build_weights(w_first, w_mid, w_last, w1f, w1, wm, w3):
    first = w_first[...].astype(F32)
    w1f[...] = jnp.zeros(w1f.shape, F32)
    for qq in range(3):
        taps = jnp.concatenate([first[3 * p + qq : 3 * p + qq + 1] for p in range(3)], axis=0)
        for late in range(3):
            for row in range(20):
                at = (late + qq) * 24 + row
                w1f[at : at + 3, late * 1280 + row * 64 : late * 1280 + row * 64 + 64] = taps
    w1[...] = w1f[...].astype(BF16)
    wm[...] = jnp.zeros(wm.shape, BF16)
    for q in range(3):
        for j in range(4):
            for p in range(3):
                wm[q, (j + p) * 64 : (j + p + 1) * 64, j * 64 : (j + 1) * 64] = w_mid[0, 3 * p + q]
    last = jnp.concatenate([w_last[...].astype(F32), jnp.zeros((9, 64), F32)], axis=1)
    last = jnp.concatenate([last, jnp.zeros((7, 128), F32)], axis=0)
    taps_t = jnp.transpose(last)[:64]
    lane = lax.broadcasted_iota(jnp.int32, (64, 128), 1)
    for q in range(3):
        base = jnp.zeros((64, 128), F32)
        for p in range(3):
            col = jnp.broadcast_to(taps_t[:, 3 * p + q : 3 * p + q + 1], (64, 128))
            base = jnp.where(lane == 2 - p, col, base)
        for row in range(18):
            rolled = pltpu.roll(base, (row - 2) % 128, axis=1)
            w3[row * 64 : (row + 1) * 64, q * 128 : (q + 1) * 128] = rolled.astype(BF16)


def hide(ext, shifted, w1, wm, h1, h2, groups, ready):
    whole = ext[...]
    for q in range(5):
        shifted[q * 24 : (q + 1) * 24, :] = pltpu.roll(whole, (3 - q) % 384, axis=1)
    shifted[120:128, :] = jnp.zeros((8, 384), F32)
    patches = jnp.transpose(shifted[...])[:TPAD].astype(BF16)
    for group in groups:
        for late in range(3):
            at = late * 1280 + group * 256
            h1[:, at : at + 256] = jnp.maximum(dot(patches, w1[:, at : at + 256]), 0.0).astype(BF16)
    for group in ready:
        depth, width = (384, 256) if group < 4 else (256, 128)
        total = None
        for q in range(3):
            at = q * 1280 + group * 256
            part = dot(h1[:, at : at + depth], wm[q, :depth, :width])
            total = part if total is None else total + part
        h2[:, group * 256 : group * 256 + width] = jnp.maximum(total, 0.0).astype(BF16)


def whiten(detrended, table_hi, table_lo):
    hi = detrended.astype(BF16)
    lo = (detrended - hi.astype(F32)).astype(BF16)
    spec = dot(hi, table_hi[...]) + (dot(lo, table_hi[...]) + dot(hi, table_lo[...]))
    re, im = spec[:, :F], spec[:, F:]
    power = re * re + im * im
    lane = lax.broadcasted_iota(jnp.int32, (C, F), 1)
    smooth = power
    for by in range(1, BAND + 1):
        smooth = smooth + jnp.where(lane >= by, pltpu.roll(power, by, axis=1), 0.0)
        smooth = smooth + jnp.where(lane < F - by, pltpu.roll(power, F - by, axis=1), 0.0)
    mean = jnp.sum(power, axis=1, keepdims=True) * (1.0 / F)
    divisor = jnp.sqrt(smooth * (1.0 / (2 * BAND + 1)) + 0.1 * mean + 1e-6)
    return jnp.concatenate([re / divisor, im / divisor], axis=1)


def kernel(
    dims, raw_at, first_at, mid_at, last_at, lower, upper, valid, dft_at, lag_at, out,
    raw, w_first, w_mid, w_last, dft, lag, in_sem,
    masked, packet, zbuf, edge_out, edge_in, xsend, xbuf, own_l, own_r,
    w1f, w1, wm, w3, ext, shifted, h1, h2, acc, spec, xall, xf, mine, got, gf, lhs,
    z_send, z_recv, e_send, e_recv, x_send, x_recv, h_send, h_recv, y_send, y_recv, o_send, o_recv,
    r_send, r_recv, n1_send, n1_recv, n2_send, n2_recv, b_send, b_recv,
):
    n_chan, n_seg, n_x = dims
    n_r = n_chan // n_x
    n_z = n_r // 2
    n_y = n_seg // 2
    half = n_chan // 2
    partners = C // n_seg
    chan, seg = lax.axis_index("chan"), lax.axis_index("seg")
    slab = lax.div(chan, n_r)
    place = lax.rem(chan, n_r)
    level = lax.div(place, 2)
    core = lax.rem(place, 2)
    side = lax.div(seg, n_y)
    column = lax.rem(seg, n_y)

    def block_at(k_x, k_z, k_c):
        return (
            lax.rem(slab + k_x, n_x) * n_r + lax.rem(level + k_z, n_z) * 2 + lax.rem(core + k_c, 2)
        )

    def seg_at(k_h, k_y):
        return lax.rem(side + k_h, 2) * n_y + lax.rem(column + k_y, n_y)

    def each(first, last, act):
        def one(k, carry):
            act(k)
            return carry
        lax.fori_loop(first, last, one, 0)

    def send(source, target, sems, at, to):
        if at is None:
            sent, landed = (sem.at[i] for sem, i in sems)
        else:
            sent, landed = (sem.at[at] for sem in sems)
        return pltpu.make_async_remote_copy(
            source, target, sent, landed, device_id=to, device_id_type=MESH
        )

    def all_of(ref, sem):
        pltpu.make_async_copy(ref, ref, sem).wait()

    arrays = [
        (raw_at, raw), (first_at, w_first),
        (mid_at, w_mid), (last_at, w_last), (dft_at, dft), (lag_at, lag),
    ]
    loads = [pltpu.make_async_copy(a, b, in_sem.at[i]) for i, (a, b) in enumerate(arrays)]
    for load in loads[:1]:
        load.start()

    barrier = pltpu.get_barrier_semaphore()

    def greet(to):
        pl.semaphore_signal(barrier, inc=1, device_id=to, device_id_type=MESH)

    for step in (1, n_seg - 1):
        each(0, n_z, lambda k: greet((block_at(0, k, 0), lax.rem(seg + step, n_seg))))
    for k_h in range(2):
        each(1 - k_h, n_z, lambda k: greet((block_at(0, k, 0), seg_at(k_h, 0))))
    for k in range(1, 2 * n_x):
        greet((block_at(k // 2, 0, k % 2), seg))
    each(1, n_y, lambda k: greet((chan, seg_at(0, k))))
    greeted = (2 * n_z - 1) + 2 * n_z + (2 * n_x - 1) + (n_y - 1)
    for load in loads[1:]:
        load.start()
    for load in loads[:1]:
        load.wait()

    live = (lax.broadcasted_iota(jnp.int32, (C, WIN), 0) < valid[0]).astype(F32)
    own = raw[...].astype(F32) * live
    masked[...] = own.astype(BF16)
    row8 = lax.broadcasted_iota(jnp.int32, (8, WIN), 0)
    goes_low, goes_high = upper[0].astype(F32), lower[0].astype(F32)
    outer = jnp.concatenate([own[13:16], own[0:3], own[0:2]], axis=0)
    outer = jnp.where(row8 == 6, goes_low, jnp.where(row8 == 7, goes_high, outer))
    packet[...] = outer.astype(BF16)
    zbuf[level] = outer.astype(BF16)
    row_t = lax.broadcasted_iota(jnp.int32, (8, 128), 0)
    lane_t = lax.broadcasted_iota(jnp.int32, (8, 128), 1)

    def packed(tile, first):
        out_rows = jnp.zeros((8, 128), F32)
        for r in range(6):
            here = (row_t == r) & (lane_t >= 4 * r) & (lane_t < 4 * r + 3)
            out_rows = jnp.where(here, pltpu.roll(tile, (4 * r - first) % 128, axis=1), out_rows)
        line = jnp.sum(out_rows, axis=0, keepdims=True)
        lane = lax.broadcasted_iota(jnp.int32, (1, 128), 1)
        return jnp.where(lane == 24, goes_low, jnp.where(lane == 25, goes_high, line))

    edge_out[0] = packed(outer[:, 128:256], 125)
    edge_out[1] = packed(outer[:, 0:128], 0)

    pl.semaphore_wait(barrier, greeted)

    def z_copy(k):
        return send(packet, zbuf.at[level], (z_send, z_recv), 0, (block_at(0, k, 0), seg))

    def e_copy(way, k):
        step = 1 if way == 0 else n_seg - 1
        to = (block_at(0, k, 0), lax.rem(seg + step, n_seg))
        return send(edge_out.at[way], edge_in.at[way, level], (e_send, e_recv), way, to)

    def x_copy(k):
        return send(xsend.at[k], xbuf.at[k], (x_send, x_recv), 0, (block_at(k // 2, 0, k % 2), seg))

    def halo_copy(way):
        source, target, step = [
            (masked.at[:, 128:256], own_l, 1),
            (masked.at[:, 0:128], own_r, n_seg - 1),
        ][way]
        return send(source, target, (h_send, h_recv), way, (chan, lax.rem(seg + step, n_seg)))

    for way in range(2):
        each(0, n_z, lambda k: e_copy(way, k).start())
    for k in sorted(range(1, n_z), key=lambda k: -min(k, n_z - k)):
        z_copy(k).start()
    for way in range(2):
        halo_copy(way).start()

    for load in loads[1:]:
        load.wait()
    build_weights(w_first, w_mid, w_last, w1f, w1, wm, w3)
    for way in range(2):
        all_of(edge_in.at[way], e_recv.at[way])
    all_of(zbuf.at[0 : n_z - 1], z_recv.at[0])
    wanted = [block_at(k // 2, 0, k % 2).astype(F32) for k in range(2 * n_x)]
    picked = [jnp.zeros((8, WIN), F32) for _ in wanted]
    for source in range(n_z):
        values = zbuf[source].astype(F32)
        goes = jnp.where(
            row8 < 3,
            jnp.broadcast_to(values[6:7], (8, WIN)),
            jnp.broadcast_to(values[7:8], (8, WIN)),
        )
        picked = [p + jnp.where(goes == w, values, 0.0) for p, w in zip(picked, wanted)]
    lane_z = lax.broadcasted_iota(jnp.int32, (n_z, 128), 1)
    for way in range(2):
        lines = edge_in[way].reshape(n_z, 128)
        goes = jnp.where(
            lane_z < 12,
            jnp.broadcast_to(lines[:, 24:25], (n_z, 128)),
            jnp.broadcast_to(lines[:, 25:26], (n_z, 128)),
        )
        lines = jnp.where(lane_z < 24, lines, 0.0)
        for k, w in enumerate(wanted):
            line = jnp.sum(jnp.where(goes == w, lines, 0.0), axis=0, keepdims=True)
            line = jnp.concatenate([line, jnp.zeros((1, 128), F32)], axis=1)
            picked[k] = jnp.where(row8 == 6 + way, jnp.broadcast_to(line, (8, WIN)), picked[k])
    for k in range(1, 2 * n_x):
        xsend[k] = picked[k].astype(BF16)
        x_copy(k).start()

    has_before = (seg > 0).astype(F32)
    has_after = (seg < n_seg - 1).astype(F32)
    for way in range(2):
        halo_copy(way).wait_recv()
    lane_c = lax.broadcasted_iota(jnp.int32, (C, 128), 1)
    own_edge = jnp.where(lane_c < 3, own_r[...].astype(F32) * has_after, 0.0)
    own_edge = jnp.where(lane_c >= 125, own_l[...].astype(F32) * has_before, own_edge)
    ext[3:19, 0:256] = own
    ext[3:19, 256:384] = own_edge
    ext[0:3, :] = jnp.zeros((3, 384), F32)
    ext[19:24, :] = jnp.zeros((5, 384), F32)
    hide(ext, shifted, w1, wm, h1, h2, (1, 2, 3), (1, 2))
    acc[...] = dot(h2[:, 256:768], w3[256:768])
    strips = picked[0]
    all_of(xbuf.at[1 : 2 * n_x], x_recv.at[0])
    for k in range(1, 2 * n_x):
        strips = strips + xbuf[k].astype(F32)
    before = jnp.broadcast_to(strips[6:7, 0:128] * has_before, (8, 128))
    after = jnp.broadcast_to(strips[7:8, 0:128] * has_after, (8, 128))
    strip_edge = jnp.zeros((8, 128), F32)
    for r in range(6):
        late = jnp.where(lane_t >= 125, pltpu.roll(before, 125 - 4 * r, axis=1), 0.0)
        both = jnp.where(lane_t < 3, pltpu.roll(after, (128 - 4 * r) % 128, axis=1), late)
        strip_edge = jnp.where(row_t == r, both, strip_edge)
    ext[0:3, 0:256] = strips[0:3]
    ext[0:3, 256:384] = strip_edge[0:3]
    ext[19:22, 0:256] = strips[3:6]
    ext[19:22, 256:384] = strip_edge[3:6]
    hide(ext, shifted, w1, wm, h1, h2, (0, 4), (0, 3, 4))
    acc[...] += dot(h2[:, 0:256], w3[0:256]) + dot(h2[:, 768:1152], w3[768:1152])
    noise_t = acc[0:256, 0:128] + acc[1:257, 128:256] + acc[2:258, 256:384]
    noise = jnp.transpose(noise_t)[:C]
    clean = (own - noise) * live
    common = jnp.sum(clean, axis=0, keepdims=True) / valid[0].astype(F32)
    detrended = (clean - common) * live
    spectra = whiten(detrended, dft.at[0], dft.at[1])
    for to in range(n_seg):
        mine[to] = spectra[to * partners : (to + 1) * partners].astype(BF16)
    spec[...] = spectra.astype(BF16)
    xall[seg] = spectra.astype(BF16)
    def y_copy(k):
        return send(spec, xall.at[seg], (y_send, y_recv), 0, (chan, seg_at(0, k)))

    def across_copy():
        return send(spec, xall.at[seg], (o_send, o_recv), 0, (chan, seg_at(1, 0)))

    def pass_on(k):
        window = xall.at[seg_at(1, 0)]
        return send(window, window, (o_send, o_recv), 1, (chan, seg_at(0, k)))

    got[place, seg] = mine[seg]

    def r_copy(k_s, k):
        to_seg = lax.rem(seg + k_s, n_seg)
        return send(
            mine.at[to_seg], got.at[place, seg], ((r_send, 0), (r_recv, k)), None,
            (block_at(0, k, 0), to_seg),
        )

    across_copy().start()
    each(1, n_y, lambda k: y_copy(k).start())
    order = sorted(range(n_z), key=lambda k: (max(k, n_z - k), k))
    for k in reversed(order):
        each(0 if k else 1, n_seg, lambda k_s: r_copy(k_s, k).start())
    def slab_copy(k_x, at, k_c):
        slot = at * 2 + core
        sent, landed = (n1_send, n1_recv) if k_x == 1 else (n2_send, n2_recv)
        return send(
            got.at[slot], got.at[k_x * n_r + slot], ((sent, 0), (landed, k_c * n_z + at)), None,
            (block_at(n_x - k_x, 0, k_c), seg),
        )

    def beside_copy(at):
        slot = at * 2 + core
        return send(
            got.at[slot], got.at[slot], ((b_send, 0), (b_recv, at)), None, (block_at(0, 0, 1), seg)
        )

    def other_needs(k_x, at):
        first = level * 2 + 1 - core
        slot = k_x * n_r + at * 2 + core
        return (slot >= first) & (slot <= first + half)

    def leaving(at, act):
        for k_c in range(2):
            act(slab_copy(1, at, k_c))

        @pl.when(at <= level)
        def _():
            act(slab_copy(2, at, 0))

        @pl.when(other_needs(2, at))
        def _():
            act(slab_copy(2, at, 1))

        @pl.when(other_needs(0, at))
        def _():
            act(beside_copy(at))

    for turn, k in enumerate(order):
        if turn == min(3, n_z - 1):
            across_copy().wait_recv()
            each(1, n_y, lambda k: pass_on(k).start())
        at = lax.rem(level + n_z - k, n_z)
        whole = got.at[at * 2 + core]
        all_of(whole if k else got.at[place, 0 : n_seg - 1], r_recv.at[k])
        leaving(at, lambda copy: copy.start())

    if n_y > 1:
        all_of(xall.at[0 : n_y - 1], y_recv.at[0])
        all_of(xall.at[0 : n_y - 1], o_recv.at[1])
    xf[...] = xall[...].astype(F32)
    def correlate(d):
        slot = place + d

        k_x, at = lax.div(slot, n_r), lax.div(lax.rem(slot, n_r), 2)
        apart = lax.rem(slot + core, 2)

        @pl.when((k_x == 0) & (apart == 1))
        def _():
            beside_copy(at).wait_recv()

        for far, landed in ((1, n1_recv), (2, n2_recv)):

            @pl.when(k_x == far)
            def _():
                all_of(got.at[slot], landed.at[apart * n_z + at])

        for w in range(n_seg):
            gf[w * partners : (w + 1) * partners, :] = got[slot, w].astype(F32)
        at = pl.multiple_of(d * C, C)
        for b in range(partners):
            cr = jnp.zeros((C, F), F32)
            ci = jnp.zeros((C, F), F32)
            for w in range(n_seg):
                row = w * partners + b
                pr = jnp.broadcast_to(gf[row : row + 1, 0:F], (C, F))
                pi = jnp.broadcast_to(gf[row : row + 1, F : 2 * F], (C, F))
                ar, ai = xf[w, :, 0:F], xf[w, :, F : 2 * F]
                cr = cr + (ar * pr + ai * pi)
                ci = ci + (ai * pr - ar * pi)
            lhs[pl.ds(at, C), b * 256 : b * 256 + F] = cr
            lhs[pl.ds(at, C), b * 256 + F : b * 256 + 2 * F] = ci

    chunk = next(c for c in range(11, 0, -1) if (half + 1) % c == 0)
    for start in range(0, half + 1, chunk):
        each(start, start + chunk, correlate)
        values = lhs[start * C : (start + chunk) * C, :]
        hi = values.astype(BF16)
        lo = (values - hi.astype(F32)).astype(BF16)
        lagged = dot(hi, lag[0]) + (dot(lo, lag[0]) + dot(hi, lag[1]))
        for d in range(chunk):
            out[start + d] = lagged[d * C : (d + 1) * C]

    for way in range(2):
        all_of(edge_in.at[way], e_send.at[way])
        halo_copy(way).wait_send()
    all_of(zbuf.at[0 : n_z - 1], z_send.at[0])
    all_of(xsend.at[1 : 2 * n_x], x_send.at[0])
    across_copy().wait_send()
    if n_y > 1:
        all_of(xall.at[0 : n_y - 1], y_send.at[0])
        all_of(xall.at[0 : n_y - 1], o_send.at[1])
    for k in range(n_z):
        all_of(mine if k else mine.at[0 : n_seg - 1], r_send.at[0])
    each(0, n_z, lambda at: leaving(at, lambda copy: copy.wait_send()))


def body(raw, w_first, w_mid, w_last, lower, upper, valid, dims):
    n_chan, n_seg, n_x = dims
    n_r = n_chan // n_x
    n_z = n_r // 2
    n_y = n_seg // 2
    half = n_chan // 2
    partners = C // n_seg
    dft = split_bf16(dft_table())
    lag = split_bf16(lag_table(partners, 1.0 / math.sqrt(n_seg * F)))
    dma = pltpu.SemaphoreType.DMA
    scratch = [
        pltpu.VMEM(raw.shape, BF16),
        pltpu.VMEM(w_first.shape, BF16),
        pltpu.VMEM(w_mid.shape, BF16),
        pltpu.VMEM(w_last.shape, BF16),
        pltpu.VMEM(dft.shape, BF16),
        pltpu.VMEM(lag.shape, BF16),
        dma((6,)),
        pltpu.VMEM((C, WIN), BF16),
        pltpu.VMEM((8, WIN), BF16),
        pltpu.VMEM((n_z, 8, WIN), BF16),
        pltpu.VMEM((2, 1, 128), F32),
        pltpu.VMEM((2, n_z, 1, 128), F32),
        pltpu.VMEM((2 * n_x, 8, WIN), BF16),
        pltpu.VMEM((2 * n_x, 8, WIN), BF16),
        pltpu.VMEM((C, 128), BF16),
        pltpu.VMEM((C, 128), BF16),
        pltpu.VMEM((128, 3840), F32),
        pltpu.VMEM((128, 3840), BF16),
        pltpu.VMEM((3, 384, 256), BF16),
        pltpu.VMEM((1152, 384), BF16),
        pltpu.VMEM((24, 384), F32),
        pltpu.VMEM((128, 384), F32),
        pltpu.VMEM((TPAD, 3840), BF16),
        pltpu.VMEM((TPAD, 1152), BF16),
        pltpu.VMEM((TPAD, 384), F32),
        pltpu.VMEM((C, 2 * F), BF16),
        pltpu.VMEM((n_seg, C, 2 * F), BF16),
        pltpu.VMEM((n_seg, C, 2 * F), F32),
        pltpu.VMEM((n_seg, partners, 2 * F), BF16),
        pltpu.VMEM((3 * n_r, n_seg, partners, 2 * F), BF16),
        pltpu.VMEM((C, 2 * F), F32),
        pltpu.VMEM(((half + 1) * C, partners * 2 * F), F32),
        dma((1,)), dma((1,)), dma((2,)), dma((2,)), dma((1,)), dma((1,)),
        dma((2,)), dma((2,)), dma((1,)), dma((1,)), dma((2,)), dma((2,)),
        dma((1,)), dma((n_z,)), dma((1,)), dma((2 * n_z,)), dma((1,)), dma((2 * n_z,)),
        dma((1,)), dma((n_z,)),
    ]
    hbm = pl.BlockSpec(memory_space=pltpu.HBM)
    smem = pl.BlockSpec(memory_space=pltpu.SMEM)
    placed = [raw, w_first, w_mid, w_last, lower, upper, valid, jnp.asarray(dft), jnp.asarray(lag)]
    placed = [
        x if x.ndim == 1 else pltpu.with_memory_space_constraint(x, pltpu.HBM) for x in placed
    ]
    lagged = pl.pallas_call(
        functools.partial(kernel, dims),
        out_shape=jax.ShapeDtypeStruct((half + 1, C, partners * NLAG), F32),
        in_specs=[hbm] * 4 + [smem] * 3 + [hbm] * 2,
        out_specs=pl.BlockSpec(memory_space=pltpu.VMEM),
        scratch_shapes=scratch,
        compiler_params=pltpu.CompilerParams(
            collective_id=0, has_side_effects=True, vmem_limit_bytes=48 << 20
        ),
    )(*placed)
    return jnp.transpose(lagged, (1, 0, 2))


def solution(mesh):
    n_chan, n_seg = mesh.shape["chan"], mesh.shape["seg"]
    dims = (n_chan, n_seg, 4)
    return jax.shard_map(
        functools.partial(body, dims=dims),
        mesh=mesh,
        in_specs=(P("chan", "seg"), P(), P(), P(), P("chan"), P("chan"), P("chan")),
        out_specs=P("chan", None, "seg"),
        check_vma=False,
    )
```
